128 devices in a mesh: tile: 16 (over y, z), intra: 8 (over x, core).
Axes of the slice: x: 4, y: 4, z: 4, core: 2. Of those that a mesh axis runs over, the one named last changes fastest.
Arguments:
- leaves: bfloat16 [65536, 256], P(('tile', 'intra')), may hold values from -6 to 6
- window_a: int32 [65536], P(('tile', 'intra')), may hold values from 0 to 127, as said below
- window_b: int32 [65536], P(('tile', 'intra')), may hold values from 0 to 127, as said below
- parent: int32 [65536], P(('tile', 'intra')), may hold values from 0 to 4095
- coarse: bfloat16 [16, 512, 256, 128], P('tile', 'intra'), may hold values from -6 to 6
- w_query: bfloat16 [2, 256, 256], replicated
- w_key: bfloat16 [2, 256, 256], replicated
- w_value: bfloat16 [2, 256, 256], replicated, may hold values from -0.375 to 0.375
- w_out: bfloat16 [2, 256, 256], replicated, may hold values from -0.375 to 0.375
- w_up: bfloat16 [2, 256, 1024], replicated, may hold values from -0.375 to 0.375
- w_down: bfloat16 [2, 1024, 256], replicated, may hold values from -0.1875 to 0.1875
- gain_attn: float32 [2, 256], replicated, may hold values from 0.25 to 1.75
- gain_mlp: float32 [2, 256], replicated, may hold values from 0.25 to 1.75
- w_expand: bfloat16 [256, 256], replicated, may hold values from -0.375 to 0.375
- w_pixels: bfloat16 [256, 512], replicated, may hold values from -0.375 to 0.375
- conv_weight: bfloat16 [3, 3, 128, 128], replicated, may hold values from -0.3125 to 0.3125
Outputs:
- field: bfloat16 [16, 512, 256, 128], P('tile', 'intra')
The draws below stay inside these ranges and needn't reach their ends.
Inputs may be any that keep to these rules, and one draw needn't show every extreme that they name: `window_a`: the leaves of one device (each aligned block of 512) name each window at most 8 times, and some window exactly 8 times from every device; every window is named by every device. `window_b`: the leaves of one partition A window name each window of partition B at most 8 times.
All inputs are finite; a program needn't handle non-finite values.
Results may differ from the reference program's by a relative error of at most 0.0045.
Values may be sent and summed in bfloat16 or wider, within the bound.
No kernel may reach another device: no remote copies, remote signals or barrier semaphores. Data moves between devices by JAX's collectives and lax.ppermute only.
A program may use at most 256 MiB of HBM per device.

```python
import jax
import jax.numpy as jnp
from jax import lax

D = 256
HEADS = 4
HEAD_DIM = 64
FF = 1024
CHANNELS = 128
LAYERS = 2
L_DEV = 512
ROW_DEV = 64
COLS = 256
WINDOWS = 128
SLOTS = 1024
LEAVES = 65536
ROWS = 512
BLOCKS = 4096
N_TILE = 16
N_INTRA = 8


def routing(key):
    base = jax.random.fold_in(key, 101)
    key_class, key_pair, key_flip, key_rows, key_table = jax.random.split(base, 5)
    mean = L_DEV // WINDOWS
    quarter = WINDOWS // 4
    order = jax.random.permutation(key_class, WINDOWS)
    base_count = jnp.full((WINDOWS,), 3 * mean // 4, jnp.int32)
    base_count = base_count.at[order[:quarter]].set(2 * mean)
    base_count = base_count.at[order[quarter:2 * quarter]].set(mean // 2)
    middle = order[2 * quarter:]

    def per_source(pair_key, flip_key):
        shuffled = jax.random.permutation(pair_key, middle)
        flips = jax.random.randint(flip_key, (shuffled.shape[0] // 2,), 0, 2)
        counts = base_count.at[shuffled[0::2]].set(jnp.where(flips == 1, mean // 2, 3 * mean // 4).astype(jnp.int32))
        counts = counts.at[shuffled[1::2]].set(jnp.where(flips == 1, mean, 3 * mean // 4).astype(jnp.int32))
        return counts
    counts = jax.vmap(per_source)(jax.random.split(key_pair, WINDOWS), jax.random.split(key_flip, WINDOWS))

    def rows_of(row_key, count_row):
        listed = jnp.repeat(jnp.arange(WINDOWS, dtype=jnp.int32), count_row, total_repeat_length=L_DEV)
        return jax.random.permutation(row_key, listed)
    dest = jax.vmap(rows_of)(jax.random.split(key_rows, WINDOWS), counts)

    def rank_of(dest_row, count_row):
        order_rows = jnp.argsort(dest_row, stable=True)
        starts = jnp.cumsum(count_row) - count_row
        ranked = jnp.arange(L_DEV, dtype=jnp.int32) - starts[dest_row[order_rows]]
        return jnp.zeros((L_DEV,), jnp.int32).at[order_rows].set(ranked.astype(jnp.int32))
    rank = jax.vmap(rank_of)(dest, counts)
    before = jnp.cumsum(counts, axis=0) - counts
    arrival = jnp.take_along_axis(before, dest, axis=1) + rank

    def table_row(row_key):
        return jax.random.permutation(row_key, WINDOWS)
    table = jax.vmap(table_row)(jax.random.split(key_table, WINDOWS))
    second = table[dest, arrival % WINDOWS]
    return (dest.reshape(LEAVES).astype(jnp.int32), second.reshape(LEAVES).astype(jnp.int32))


def draw_window_a(key, part):
    return routing(key)[0]


def draw_window_b(key, part):
    return routing(key)[1]


def query_key(key):
    base = jax.random.fold_in(key, 202)
    first, second = jax.random.split(base)
    shape = (LAYERS, D, D)
    key_part = jax.random.normal(first, shape, jnp.float32) * D ** (-0.5)
    noise = jax.random.normal(second, shape, jnp.float32) * D ** (-0.5)
    query_part = noise
    return (query_part, key_part)


def draw_w_query(key, part):
    return query_key(key)[0].astype(jnp.bfloat16)


def draw_w_key(key, part):
    return query_key(key)[1].astype(jnp.bfloat16)


def set_ends(drawn, rng, low, top_value):
    longest = drawn.shape.index(max(drawn.shape))
    spots = []
    for shift in (0, 1):
        where = [jax.random.randint(jax.random.fold_in(rng, axis), (), 0, length) for axis, length in enumerate(drawn.shape)]
        where[longest] = (where[longest] + shift) % drawn.shape[longest]
        spots.append(tuple(where))
    return drawn.at[spots[0]].set(low).at[spots[1]].set(top_value)


def level_of(key, dims, cuts, least, top_value):
    level, own = 1.0, jax.random.fold_in(key, 6)
    for dim, blocks in cuts:
        draws = jnp.exp(jax.random.uniform(jax.random.fold_in(own, dim), (blocks,), jnp.float32, least / len(cuts), top_value / len(cuts)))
        level = level * jnp.repeat(draws, dims[dim] // blocks).reshape([-1 if axis == dim else 1 for axis in range(len(dims))])
    return level


def centred(key, extent, width, reach, cuts=(), kind=jnp.bfloat16):
    loudness = level_of(key, extent, cuts, -0.22, 0.18) if cuts else 1.0
    drawn = jax.random.normal(key, extent, jnp.float32) * width * loudness
    return jnp.minimum(jnp.maximum(drawn, -reach), reach).astype(kind)


def setup_inputs(seed: int = 0) -> dict:
    key_of = jax.random.split(jax.random.key(seed), 17)
    leaves = centred(key_of[0], (LEAVES, D), 1.0, 6.0, ((0, 128),))
    window_a = draw_window_a(jax.random.fold_in(key_of[16], 71), 0)
    window_b = draw_window_b(jax.random.fold_in(key_of[16], 71), 0)
    parent = set_ends(jax.random.randint(key_of[3], (LEAVES,), 0, BLOCKS), jax.random.fold_in(key_of[3], 1), 0, BLOCKS - 1).astype(jnp.int32)
    coarse = centred(key_of[4], (N_TILE, ROWS, COLS, CHANNELS), 1.0, 6.0, ((0, 16), (1, 8)))
    w_query = draw_w_query(jax.random.fold_in(key_of[16], 71), 0)
    w_key = draw_w_key(jax.random.fold_in(key_of[16], 71), 0)
    w_value = centred(key_of[7], (LAYERS, D, D), D ** -0.5, 0.375)
    w_out = centred(key_of[8], (LAYERS, D, D), D ** -0.5, 0.375)
    w_up = centred(key_of[9], (LAYERS, D, FF), D ** -0.5, 0.375)
    w_down = centred(key_of[10], (LAYERS, FF, D), FF ** -0.5, 0.1875)
    gain_attn = jnp.clip(1.0 + 0.15 * jax.random.normal(key_of[11], (LAYERS, D), jnp.float32), 0.25, 1.75)
    gain_mlp = jnp.clip(1.0 + 0.15 * jax.random.normal(key_of[12], (LAYERS, D), jnp.float32), 0.25, 1.75)
    w_expand = centred(key_of[13], (D, D), D ** -0.5, 0.375)
    w_pixels = centred(key_of[14], (D, 4 * CHANNELS), (D * max(1, L_DEV // BLOCKS)) ** -0.5, 0.375)
    conv_weight = centred(key_of[15], (3, 3, CHANNELS, CHANNELS), (3 * CHANNELS) ** -0.5, 0.3125)
    return dict(leaves=leaves, window_a=window_a, window_b=window_b, parent=parent, coarse=coarse, w_query=w_query, w_key=w_key, w_value=w_value, w_out=w_out, w_up=w_up, w_down=w_down, gain_attn=gain_attn, gain_mlp=gain_mlp, w_expand=w_expand, w_pixels=w_pixels, conv_weight=conv_weight)


EPSILON = 1e-06
NEGATIVE = -1e+30

def rms_scale(values, gain):
    mean_sq = lax.optimization_barrier(jnp.mean(values * values, axis=-1, keepdims=True))
    return (values * lax.rsqrt(mean_sq + EPSILON) * gain).astype(jnp.bfloat16)

def attend_block(query, keys, values_v, live):
    scores = jnp.einsum('rhe,she->hrs', query.astype(jnp.float32), keys.astype(jnp.float32)) * HEAD_DIM ** (-0.5)
    scores = jnp.where(live[None, None, :], scores, NEGATIVE)
    top = lax.optimization_barrier(jnp.max(scores, axis=-1, keepdims=True))
    weights = jnp.exp(scores - top)
    total = lax.optimization_barrier(jnp.sum(weights, axis=-1, keepdims=True))
    probs = (weights / total).astype(jnp.bfloat16)
    return jnp.einsum('hrs,she->rhe', probs.astype(jnp.float32), values_v.astype(jnp.float32))

def window_layer(rows, live, params):
    w_query, w_key, w_value, w_out, w_up, w_down, gain_one, gain_two = params
    count = rows.shape[0]
    block_rows = 512 if count % 512 == 0 else count
    wide = rows.astype(jnp.float32)
    normed = rms_scale(wide, gain_one)
    query = jnp.dot(normed, w_query, preferred_element_type=jnp.float32).astype(jnp.bfloat16)
    keys = jnp.dot(normed, w_key, preferred_element_type=jnp.float32).astype(jnp.bfloat16)
    values_v = jnp.dot(normed, w_value, preferred_element_type=jnp.float32).astype(jnp.bfloat16)
    keys = keys.reshape(count, HEADS, HEAD_DIM)
    values_v = values_v.reshape(count, HEADS, HEAD_DIM)
    blocked = query.reshape(count // block_rows, block_rows, HEADS, HEAD_DIM)

    def one_block(query_block):
        return attend_block(query_block, keys, values_v, live)
    attended = lax.map(one_block, blocked).reshape(count, HEADS * HEAD_DIM).astype(jnp.bfloat16)
    hidden = wide + jnp.dot(attended, w_out, preferred_element_type=jnp.float32)
    normed_two = rms_scale(hidden, gain_two)
    upward = jax.nn.gelu(jnp.dot(normed_two, w_up, preferred_element_type=jnp.float32)).astype(jnp.bfloat16)
    return (hidden + jnp.dot(upward, w_down, preferred_element_type=jnp.float32)).astype(jnp.bfloat16)

def windows_pass(rows, window, params):
    order = jnp.argsort(window, stable=True).astype(jnp.int32)
    sorted_rows = rows[order]
    sorted_win = window[order]
    counts = jnp.zeros((WINDOWS,), jnp.int32).at[window].add(1)
    starts = (jnp.cumsum(counts) - counts).astype(jnp.int32)
    padded = jnp.concatenate([sorted_rows, jnp.zeros((SLOTS, D), rows.dtype)], 0)

    def one_window(index):
        block = lax.dynamic_slice_in_dim(padded, starts[index], SLOTS, 0)
        live = jnp.arange(SLOTS, dtype=jnp.int32) < counts[index]
        return window_layer(block, live, params)
    results = lax.map(one_window, jnp.arange(WINDOWS, dtype=jnp.int32))
    offsets = jnp.arange(LEAVES, dtype=jnp.int32) - starts[sorted_win]
    sorted_out = results[sorted_win, offsets]
    return jnp.zeros_like(rows).at[order].set(sorted_out)

def reference(leaves, window_a, window_b, parent, coarse, w_query, w_key, w_value, w_out, w_up, w_down, gain_attn, gain_mlp, w_expand, w_pixels, conv_weight):
    first = (w_query[0], w_key[0], w_value[0], w_out[0], w_up[0], w_down[0], gain_attn[0], gain_mlp[0])
    second = (w_query[1], w_key[1], w_value[1], w_out[1], w_up[1], w_down[1], gain_attn[1], gain_mlp[1])
    layer_one = windows_pass(leaves, window_a, first)
    layer_two = windows_pass(layer_one, window_b, second)
    expanded = jax.nn.gelu(jnp.dot(layer_two, w_expand, preferred_element_type=jnp.float32)).astype(jnp.bfloat16)
    pixels = jnp.dot(expanded, w_pixels, preferred_element_type=jnp.float32).astype(jnp.bfloat16)
    segment = jnp.arange(LEAVES, dtype=jnp.int32) // L_DEV * BLOCKS + parent
    summed = jax.ops.segment_sum(pixels.astype(jnp.float32), segment, num_segments=WINDOWS * BLOCKS)
    summed = summed.reshape(N_TILE, N_INTRA, ROW_DEV // 2, COLS // 2, 2, 2, CHANNELS)
    summed = summed.transpose(0, 1, 2, 4, 3, 5, 6).reshape(N_TILE, ROWS, COLS, CHANNELS)
    padded = jnp.pad(coarse, ((0, 0), (1, 1), (1, 1), (0, 0)))
    conv = jnp.zeros((N_TILE, ROWS, COLS, CHANNELS), jnp.float32)
    for row_off in range(3):
        for col_off in range(3):
            window_px = padded[:, row_off:row_off + ROWS, col_off:col_off + COLS, :]
            conv = conv + jnp.einsum('thwc,cd->thwd', window_px.astype(jnp.float32), conv_weight[row_off, col_off].astype(jnp.float32))
    return (conv + summed).astype(jnp.bfloat16)
```

```python
import functools
import math

import jax
import jax.numpy as jnp
from jax import lax
from jax.experimental import pallas as pl
from jax.experimental.pallas import tpu as pltpu
from jax.sharding import PartitionSpec as P

HEADS = 4
HEAD_DIM = 64
EPSILON = 1e-06
NEGATIVE = -1e30
LOG2E = math.log2(math.e)
D = 256
LANES = 128
WIDE = D + LANES
DEVICES = 128
CAP = 8
SLOTS = DEVICES * CAP
LEAVES = 512
RET = 16
BACK = DEVICES * RET
TILE = 256
FF = 1024
F32 = jnp.float32
BF16 = jnp.bfloat16
I32 = jnp.int32

VMEM = pl.BlockSpec(memory_space=pltpu.VMEM)


def iota(shape, dim):
    return lax.broadcasted_iota(I32, shape, dim)


def fiota(shape, dim):
    return iota(shape, dim).astype(F32)


def dot(a, b):
    return jnp.dot(a, b, preferred_element_type=F32)


def dot_nt(a, b):
    return lax.dot_general(a, b, (((1,), (1,)), ((), ())), preferred_element_type=F32)


def columns(row, count):
    return jnp.broadcast_to(row, (LANES, count)).T


def onehot_rows(first, rows, targets):
    want = iota((rows, targets.shape[1]), 0) + first
    return jnp.where(want == targets, 1.0, 0.0).astype(BF16)


def send_kernel(leaves_ref, wa_ref, wb_ref, out_ref, ret_ref):
    a_row = wa_ref[...].astype(F32)
    b_row = wb_ref[...].astype(F32)
    a_col = columns(a_row, LEAVES)
    b_col = columns(b_row, LEAVES)
    l_col = fiota((LEAVES, LANES), 0)
    key_col = a_col * LEAVES + l_col
    slots = []
    ranks = []
    for part in range(LEAVES // LANES):
        lanes = slice(part * LANES, (part + 1) * LANES)
        ar = a_row[:, lanes]
        br = b_row[:, lanes]
        lr = fiota((1, LANES), 1) + part * LANES
        same_a = jnp.where(a_col == ar, jnp.where(l_col < lr, 1.0, 0.0), 0.0)
        same_b = jnp.where(b_col == br, jnp.where(key_col < ar * LEAVES + lr, 1.0, 0.0), 0.0)
        slots.append(ar * CAP + jnp.sum(same_a, axis=0, keepdims=True))
        ranks.append(jnp.sum(same_b, axis=0, keepdims=True))
    slot = jnp.concatenate(slots, axis=1).astype(I32)
    rank = jnp.concatenate(ranks, axis=1)
    turn = jnp.floor(rank * (1.0 / RET))
    ret = b_row * RET + (rank - turn * RET) + turn * BACK
    ret_ref[...] = jnp.broadcast_to(ret, (8, LEAVES)).astype(I32)
    rounds = jnp.max(turn) + 1.0
    lane = iota((LEAVES, LANES), 1)
    extra = jnp.where(lane == 0, b_col + 1.0, jnp.where(lane == 1, rounds, 0.0)).astype(BF16)
    for first in range(0, SLOTS, TILE):
        hot = onehot_rows(first, TILE, slot)
        out_ref[first : first + TILE, :D] = dot(hot, leaves_ref[...]).astype(BF16)
        out_ref[first : first + TILE, D:] = dot(hot, extra).astype(BF16)


def tags_of(x_ref):
    tags = x_ref[:, D:]
    picks = jnp.where(iota((8, LANES), 0) == iota((8, LANES), 1), 1.0, 0.0).astype(BF16)
    rows = dot_nt(picks, tags)
    spread = jnp.where(iota((LANES, LANES), 0) == 0, 1.0, 0.0).astype(BF16)
    return rows[0:1, :], dot(tags, spread), jnp.max(rows[1:2, :])


def ranks_of(tag_row, tag_col):
    ranks = []
    for part in range(SLOTS // LANES):
        row = tag_row[:, part * LANES : (part + 1) * LANES]
        block = tag_col[part * LANES : (part + 1) * LANES, :]
        before = iota((LANES, LANES), 0) < iota((LANES, LANES), 1)
        hits = jnp.where(before, jnp.where(block == row, 1.0, 0.0), 0.0)
        rank = jnp.sum(hits, axis=0, keepdims=True)
        if part:
            above = jnp.where(tag_col[: part * LANES, :] == row, 1.0, 0.0)
            rank = rank + jnp.sum(above, axis=0, keepdims=True)
        ranks.append(rank)
    return jnp.concatenate(ranks, axis=1)


def rms(values, gain):
    mean_sq = jnp.mean(values * values, axis=-1, keepdims=True)
    return (values * lax.rsqrt(mean_sq + EPSILON) * gain).astype(BF16)


def layer(layer_index, x_ref, tag_row, weights, y_ref, q_ref, k_ref, v_ref):
    wq, wk, wv, wo, wu, wd, gain_one, gain_two = weights
    one = gain_one[layer_index : layer_index + 1, :]
    two = gain_two[layer_index : layer_index + 1, :]
    head_of = iota((TILE, D), 1) // HEAD_DIM

    def project(step, _):
        rows = pl.ds(pl.multiple_of(step * TILE, TILE), TILE)
        normed = rms(x_ref[rows, :D].astype(F32), one)
        q_ref[rows, :] = dot(normed, wq[0]).astype(BF16) * jnp.asarray(HEAD_DIM**-0.5, BF16)
        k_ref[rows, :] = dot(normed, wk[0]).astype(BF16)
        value = dot(normed, wv[0]).astype(BF16)
        for head in range(HEADS):
            v_ref[head, rows, :] = jnp.where(head_of == head, value, jnp.asarray(1, BF16))
        return 0

    lax.fori_loop(0, SLOTS // TILE, project, 0)
    live = tag_row > 0.0

    def attend(step, _):
        rows = pl.ds(pl.multiple_of(step * TILE, TILE), TILE)
        query = q_ref[rows, :]
        top = jnp.zeros((TILE, D), F32)
        total = jnp.zeros((TILE, D), F32)
        for head in range(HEADS):
            own = jnp.where(head_of == head, query, jnp.asarray(0, BF16))
            scores = dot_nt(own, k_ref[...])
            scores = jnp.where(live, scores, NEGATIVE)
            peak = jnp.max(scores, axis=-1, keepdims=True)
            probs = jnp.exp2((scores - peak) * LOG2E).astype(BF16)
            mixed = dot(probs, v_ref[head])
            top = jnp.where(head_of == head, mixed, top)
            total = jnp.where(head_of == (head + 1) % HEADS, mixed, total)
        total = pltpu.roll(total, D - HEAD_DIM, 1)
        att = (top / total).astype(BF16)
        hidden = x_ref[rows, :D].astype(F32) + dot(att, wo[0])
        up = jax.nn.gelu(dot(rms(hidden, two), wu[0])).astype(BF16)
        y_ref[rows, :] = (hidden + dot(up, wd[0])).astype(BF16)
        return 0

    lax.fori_loop(0, SLOTS // TILE, attend, 0)


def layer_a_kernel(x_ref, *refs):
    weights, (out_ref, y_ref, q_ref, k_ref, v_ref) = refs[:8], refs[8:]
    tag_row, tag_col, rounds = tags_of(x_ref)
    layer(0, x_ref, tag_row, weights, y_ref, q_ref, k_ref, v_ref)
    slot = (tag_row - 1.0) * CAP + ranks_of(tag_row, tag_col)
    slot = jnp.where(tag_row > 0.0, slot, -1.0).astype(I32)
    lane = iota((SLOTS, LANES), 1)
    home = iota((SLOTS, LANES), 0) // CAP + 1
    extra = jnp.where(lane == 0, home.astype(F32), 0.0).astype(BF16)
    for first in range(0, SLOTS, TILE):
        hot = onehot_rows(first, TILE, slot)
        out_ref[first : first + TILE, :D] = dot(hot, y_ref[...]).astype(BF16)
        tail = jnp.where(lane[:TILE] == 1, rounds, dot(hot, extra))
        out_ref[first : first + TILE, D:] = tail.astype(BF16)


def layer_b_kernel(x_ref, *refs):
    weights, (out_ref, y_ref, slot_ref, rounds_ref, q_ref, k_ref, v_ref) = refs[:8], refs[8:]
    tag_row, tag_col, rounds = tags_of(x_ref)
    layer(1, x_ref, tag_row, weights, y_ref, q_ref, k_ref, v_ref)
    rank = ranks_of(tag_row, tag_col)
    turn = jnp.floor(rank * (1.0 / RET))
    slot = (tag_row - 1.0) * RET + (rank - turn * RET) + turn * BACK
    slot = jnp.where(tag_row > 0.0, slot, -1.0).astype(I32)
    slot_ref[...] = jnp.broadcast_to(slot, (8, SLOTS))
    rounds_ref[...] = jnp.full((8, LANES), rounds, F32).astype(I32)
    for first in range(0, BACK, TILE):
        hot = onehot_rows(first, TILE, slot)
        out_ref[first : first + TILE, :] = dot(hot, y_ref[...]).astype(BF16)


def call_layer(kernel, layer_index, out_shape, x, weights):
    own = lambda *shape: pl.BlockSpec((1,) + shape, lambda i: (layer_index, 0, 0))
    whole = lambda *shape: pl.BlockSpec(shape, lambda i: (0,) * len(shape))
    specs = [whole(SLOTS, WIDE)] + [own(D, D)] * 4 + [own(D, FF), own(FF, D), whole(2, D), whole(2, D)]
    scratch = [
        pltpu.VMEM((SLOTS, D), BF16),
        pltpu.VMEM((SLOTS, D), BF16),
        pltpu.VMEM((HEADS, SLOTS, D), BF16),
    ]
    if len(out_shape) == 1:
        scratch = [pltpu.VMEM((SLOTS, D), BF16)] + scratch
    return pl.pallas_call(
        kernel,
        grid=(1,),
        out_shape=out_shape,
        in_specs=specs,
        out_specs=[whole(*shape.shape) for shape in out_shape],
        scratch_shapes=scratch,
        compiler_params=pltpu.CompilerParams(vmem_limit_bytes=40 * 2**20),
        cost_estimate=pl.CostEstimate(flops=6 * 10**9, bytes_accessed=4 * 2**20, transcendentals=5 * 2**20),
    )(x, *weights)


def resend_kernel(turn_ref, y_ref, slot_ref, out_ref):
    slot = slot_ref[0:1, :] - turn_ref[0] * BACK
    for first in range(0, BACK, TILE):
        hot = onehot_rows(first, TILE, slot)
        out_ref[first : first + TILE, :] = dot(hot, y_ref[...]).astype(BF16)


def gathered(want, back_ref):
    parts = []
    for first in range(0, LEAVES, LANES):
        block = want[first : first + LANES, :]
        hot = jnp.concatenate(
            [
                jnp.where(block == iota((LANES, LANES), 1) + lanes, 1.0, 0.0).astype(BF16)
                for lanes in range(0, BACK, LANES)
            ],
            axis=1,
        )
        parts.append(dot(hot, back_ref[...]))
    return jnp.concatenate(parts, axis=0)


def regather_kernel(turn_ref, back_ref, want_ref, held_ref, out_ref):
    rows = gathered(want_ref[...] - turn_ref[0] * BACK, back_ref)
    out_ref[...] = (held_ref[...].astype(F32) + rows).astype(BF16)


def order_kernel(ret_ref, parent_ref, want_ref, pixel_ref, start_ref):
    parent = parent_ref[...].astype(F32)
    ret = ret_ref[0:1, :].astype(F32)
    p_col = columns(parent, LEAVES)
    l_col = fiota((LEAVES, LANES), 0)
    parts = []
    for part in range(LEAVES // LANES):
        pr = parent[:, part * LANES : (part + 1) * LANES]
        lr = fiota((1, LANES), 1) + part * LANES
        less = jnp.where(p_col * LEAVES + l_col < pr * LEAVES + lr, 1.0, 0.0)
        parts.append(jnp.sum(less, axis=0, keepdims=True))
    place = jnp.concatenate(parts, axis=1)
    hit = place == fiota((LEAVES, LEAVES), 0)
    want = jnp.sum(jnp.where(hit, ret, 0.0), axis=1, keepdims=True)
    want_ref[...] = jnp.broadcast_to(want, (LEAVES, LANES)).astype(I32)
    place_col = columns(place, LEAVES)
    rows = []
    for part in range(LEAVES // LANES):
        inside = place_col == fiota((1, LANES), 1) + part * LANES
        moved = 2.0 * jnp.sum(jnp.where(inside, p_col, 0.0), axis=0, keepdims=True)
        rows.append(jnp.concatenate([moved, moved + 1.0], axis=1))
    pixel_ref[...] = jnp.concatenate(rows + rows, axis=0).astype(I32)
    below = jnp.where(p_col < fiota((1, LANES), 1) * LANES, 1.0, 0.0)
    start_ref[...] = jnp.broadcast_to(jnp.sum(below, axis=0, keepdims=True), (8, LANES)).astype(I32)


def call_order(ret, parent):
    return pl.pallas_call(
        order_kernel,
        out_shape=[
            jax.ShapeDtypeStruct((LEAVES, LANES), I32),
            jax.ShapeDtypeStruct((8, TILE), I32),
            jax.ShapeDtypeStruct((8, LANES), I32),
        ],
        in_specs=[VMEM, VMEM],
        out_specs=[VMEM, VMEM, VMEM],
        compiler_params=pltpu.CompilerParams(vmem_limit_bytes=24 * 2**20),
        cost_estimate=pl.CostEstimate(flops=10**9, bytes_accessed=2**20, transcendentals=0),
    )(ret, parent)


STRIP = 8


def conv_kernel(count, main_ref, above_ref, below_ref, head_ref, foot_ref, weight_ref, out_ref, w_ref):
    step = pl.program_id(0)

    @pl.when(step == 0)
    def _():
        zero = jnp.zeros((LANES, LANES), BF16)
        for b in range(3):
            for row in range(4):
                for r in range(2):
                    block = weight_ref[row - r, b] if 0 <= row - r < 3 else zero
                    w_ref[b, row * LANES : (row + 1) * LANES, r * LANES : (r + 1) * LANES] = block

    above = jnp.where(step == 0, head_ref[0, 0], above_ref[0, 0])
    below = jnp.where(step == count - 1, foot_ref[0, 0], below_ref[0, 0])
    rows = [above] + [main_ref[0, r] for r in range(STRIP)] + [below]
    column = iota((TILE, TILE), 0)
    for pair in range(STRIP // 2):
        wide = jnp.concatenate(rows[2 * pair : 2 * pair + 4], axis=1)
        left = pltpu.roll(dot(wide, w_ref[0]), 1, 0)
        right = pltpu.roll(dot(wide, w_ref[2]), TILE - 1, 0)
        both = dot(wide, w_ref[1])
        both = both + jnp.where(column == 0, 0.0, left) + jnp.where(column == TILE - 1, 0.0, right)
        out_ref[0, 2 * pair] = both[:, :LANES].astype(BF16)
        out_ref[0, 2 * pair + 1] = both[:, LANES:].astype(BF16)


def call_conv(coarse, head, foot, weight):
    rows, cols, channels = coarse.shape[1:]
    count = rows // STRIP
    single = (1, 1, cols, channels)
    return pl.pallas_call(
        functools.partial(conv_kernel, count),
        grid=(count,),
        out_shape=jax.ShapeDtypeStruct(coarse.shape, BF16),
        in_specs=[
            pl.BlockSpec((1, STRIP, cols, channels), lambda i: (0, i, 0, 0)),
            pl.BlockSpec(single, lambda i: (0, jnp.maximum(i * STRIP - 1, 0), 0, 0)),
            pl.BlockSpec(single, lambda i: (0, jnp.minimum(i * STRIP + STRIP, rows - 1), 0, 0)),
            pl.BlockSpec(single, lambda i: (0, 0, 0, 0)),
            pl.BlockSpec(single, lambda i: (0, 0, 0, 0)),
            pl.BlockSpec(weight.shape, lambda i: (0, 0, 0, 0)),
        ],
        out_specs=pl.BlockSpec((1, STRIP, cols, channels), lambda i: (0, i, 0, 0)),
        scratch_shapes=[pltpu.VMEM((3, 4 * LANES, 2 * LANES), BF16)],
        compiler_params=pltpu.CompilerParams(vmem_limit_bytes=24 * 2**20),
        cost_estimate=pl.CostEstimate(flops=6 * 10**9, bytes_accessed=8 * 2**20, transcendentals=0),
    )(coarse, coarse, coarse, head, foot, weight)


def field_kernel(start_ref, conv_ref, back_ref, held_ref, want_ref, pixel_ref, we_ref, wp_ref, out_ref, pix_ref, acc_ref):
    step = pl.program_id(0)

    @pl.when(step == 0)
    def _():
        leaf = (gathered(want_ref[...], back_ref) + held_ref[...].astype(F32)).astype(BF16)
        expanded = jax.nn.gelu(dot(leaf, we_ref[...])).astype(BF16)
        pixels = dot(expanded, wp_ref[...]).astype(BF16)
        for part in range(LEAVES // LANES):
            leaves = slice(part * LANES, (part + 1) * LANES)
            for c in range(2):
                for r in range(2):
                    block = pixels[leaves, (2 * r + c) * LANES : (2 * r + c + 1) * LANES]
                    pix_ref[part, c * LANES : (c + 1) * LANES, r * LANES : (r + 1) * LANES] = block

    for pair in range(STRIP // 2):
        index = step * (STRIP // 2) + pair
        acc_ref[:, :LANES] = conv_ref[0, 2 * pair].astype(F32)
        acc_ref[:, LANES:] = conv_ref[0, 2 * pair + 1].astype(F32)

        def add(part, _):
            target = pixel_ref[pl.ds(part, 1), :] - index * TILE
            hot = jnp.where(iota((TILE, TILE), 0) == target, 1.0, 0.0).astype(BF16)
            acc_ref[...] += dot(hot, pix_ref[part])
            return 0

        low = start_ref[index] // LANES
        high = (start_ref[index + 1] + LANES - 1) // LANES
        lax.fori_loop(low, high, add, 0)
        out_ref[0, 2 * pair] = acc_ref[:, :LANES].astype(BF16)
        out_ref[0, 2 * pair + 1] = acc_ref[:, LANES:].astype(BF16)


def call_field(starts, conv, back, held, want, pixel, w_expand, w_pixels):
    rows, cols, channels = conv.shape[1:]
    whole = lambda *shape: pl.BlockSpec(shape, lambda i, s: (0,) * len(shape))
    strip = pl.BlockSpec((1, STRIP, cols, channels), lambda i, s: (0, i, 0, 0))
    return pl.pallas_call(
        field_kernel,
        grid_spec=pltpu.PrefetchScalarGridSpec(
            num_scalar_prefetch=1,
            grid=(rows // STRIP,),
            in_specs=[
                strip,
                whole(BACK, D),
                whole(LEAVES, D),
                whole(LEAVES, LANES),
                whole(8, TILE),
                whole(D, D),
                whole(D, 4 * LANES),
            ],
            out_specs=strip,
            scratch_shapes=[pltpu.VMEM((LEAVES // LANES, TILE, TILE), BF16), pltpu.VMEM((TILE, TILE), F32)],
        ),
        out_shape=jax.ShapeDtypeStruct(conv.shape, BF16),
        compiler_params=pltpu.CompilerParams(vmem_limit_bytes=32 * 2**20),
        cost_estimate=pl.CostEstimate(flops=2 * 10**9, bytes_accessed=10 * 2**20, transcendentals=2**17),
    )(starts, conv, back, held, want, pixel, w_expand, w_pixels)


def exchange(rows, capacity):
    width = rows.shape[1]
    blocks = rows.reshape(DEVICES, capacity, width)
    moved = lax.all_to_all(blocks, ("tile", "intra"), split_axis=0, concat_axis=0, tiled=True)
    return moved.reshape(DEVICES * capacity, width)


def shards(
    leaves,
    window_a,
    window_b,
    parent,
    coarse,
    w_query,
    w_key,
    w_value,
    w_out,
    w_up,
    w_down,
    gain_attn,
    gain_mlp,
    w_expand,
    w_pixels,
    conv_weight,
):
    weights = (w_query, w_key, w_value, w_out, w_up, w_down, gain_attn, gain_mlp)
    count = lax.axis_size("intra")
    rows = coarse.shape[1]
    head = lax.ppermute(coarse[:, rows - 1 :], "intra", [(i, i + 1) for i in range(count - 1)])
    foot = lax.ppermute(coarse[:, :1], "intra", [(i + 1, i) for i in range(count - 1)])
    sent, ret = pl.pallas_call(
        send_kernel,
        out_shape=[jax.ShapeDtypeStruct((SLOTS, WIDE), BF16), jax.ShapeDtypeStruct((8, LEAVES), I32)],
        in_specs=[VMEM] * 3,
        out_specs=[VMEM] * 2,
        compiler_params=pltpu.CompilerParams(vmem_limit_bytes=24 * 2**20),
        cost_estimate=pl.CostEstimate(flops=10**9, bytes_accessed=2**20, transcendentals=0),
    )(leaves, window_a.reshape(1, LEAVES), window_b.reshape(1, LEAVES))
    rows_a = exchange(sent, CAP)
    (sent_b,) = call_layer(
        layer_a_kernel, 0, [jax.ShapeDtypeStruct((SLOTS, WIDE), BF16)], rows_a, weights
    )
    rows_b = exchange(sent_b, CAP)
    home, y, slot, rounds = call_layer(
        layer_b_kernel,
        1,
        [
            jax.ShapeDtypeStruct((BACK, D), BF16),
            jax.ShapeDtypeStruct((SLOTS, D), BF16),
            jax.ShapeDtypeStruct((8, SLOTS), I32),
            jax.ShapeDtypeStruct((8, LANES), I32),
        ],
        rows_b,
        weights,
    )
    back = exchange(home, RET)
    conv = call_conv(coarse, head, foot, conv_weight)
    want, pixel, starts = call_order(ret, parent.reshape(1, LEAVES))
    total = rounds[0, 0]

    def more(state):
        return state[0] < total

    def again(state):
        turn, held = state
        index = turn.reshape(1)
        smem = pl.BlockSpec(memory_space=pltpu.SMEM)
        part = pl.pallas_call(
            resend_kernel,
            out_shape=jax.ShapeDtypeStruct((BACK, D), BF16),
            in_specs=[smem, VMEM, VMEM],
            out_specs=VMEM,
        )(index, y, slot)
        held = pl.pallas_call(
            regather_kernel,
            out_shape=jax.ShapeDtypeStruct((LEAVES, D), BF16),
            in_specs=[smem, VMEM, VMEM, VMEM],
            out_specs=VMEM,
        )(index, exchange(part, RET), want, held)
        return turn + 1, held

    _, held = lax.while_loop(more, again, (jnp.asarray(1, I32), jnp.zeros((LEAVES, D), BF16)))
    return call_field(starts[0], conv, back, held, want, pixel, w_expand, w_pixels)


def solution(mesh):
    placed = (
        P(("tile", "intra"), None),
        P(("tile", "intra")),
        P(("tile", "intra")),
        P(("tile", "intra")),
        P("tile", "intra", None, None),
    ) + (P(),) * 11
    return jax.shard_map(
        shards,
        mesh=mesh,
        in_specs=placed,
        out_specs=P("tile", "intra", None, None),
        check_vma=False,
    )
```

```python
import functools
import math

import jax
import jax.numpy as jnp
from jax import lax
from jax.experimental import pallas as pl
from jax.experimental.pallas import tpu as pltpu
from jax.sharding import PartitionSpec as P

HEADS = 4
HEAD_DIM = 64
EPSILON = 1e-06
NEGATIVE = -1e30
LOG2E = math.log2(math.e)
D = 256
LANES = 128
WIDE = D + LANES
DEVICES = 128
CAP = 8
SLOTS = DEVICES * CAP
LEAVES = 512
RET = 16
BACK = DEVICES * RET
FEW = 640
GROUP = 64
ALIGN = 16
TILE = 256
FF = 1024
F32 = jnp.float32
BF16 = jnp.bfloat16
I32 = jnp.int32

VMEM = pl.BlockSpec(memory_space=pltpu.VMEM)


def kept(array):
    return pltpu.with_memory_space_constraint(array, pltpu.HBM)


def iota(shape, dim):
    return lax.broadcasted_iota(I32, shape, dim)


def fiota(shape, dim):
    return iota(shape, dim).astype(F32)


def dot(a, b):
    return jnp.dot(a, b, preferred_element_type=F32)


def dot_nt(a, b):
    return lax.dot_general(a, b, (((1,), (1,)), ((), ())), preferred_element_type=F32)


def columns(row, count):
    return jnp.broadcast_to(row, (LANES, count)).T


def onehot_rows(first, rows, targets):
    want = iota((rows, targets.shape[1]), 0) + first
    return jnp.where(want == targets, 1.0, 0.0).astype(BF16)


def send_kernel(leaves_hbm, wa_hbm, wb_hbm, out_ref, ret_ref, leaves_ref, wa_ref, wb_ref, sems):
    moves = [
        pltpu.make_async_copy(source, target, sems.at[index])
        for index, (source, target) in enumerate(((wa_hbm, wa_ref), (wb_hbm, wb_ref), (leaves_hbm, leaves_ref)))
    ]
    for move in moves:
        move.start()
    moves[0].wait()
    moves[1].wait()
    a_row = wa_ref[...].astype(F32)
    b_row = wb_ref[...].astype(F32)
    a_col = columns(a_row, LEAVES)
    b_col = columns(b_row, LEAVES)
    l_col = fiota((LEAVES, LANES), 0)
    key_col = a_col * LEAVES + l_col
    slots = []
    ranks = []
    for part in range(LEAVES // LANES):
        lanes = slice(part * LANES, (part + 1) * LANES)
        ar = a_row[:, lanes]
        br = b_row[:, lanes]
        lr = fiota((1, LANES), 1) + part * LANES
        same_a = jnp.where(a_col == ar, jnp.where(l_col < lr, 1.0, 0.0), 0.0)
        same_b = jnp.where(b_col == br, jnp.where(key_col < ar * LEAVES + lr, 1.0, 0.0), 0.0)
        slots.append(ar * CAP + jnp.sum(same_a, axis=0, keepdims=True))
        ranks.append(jnp.sum(same_b, axis=0, keepdims=True))
    slot = jnp.concatenate(slots, axis=1).astype(I32)
    rank = jnp.concatenate(ranks, axis=1)
    turn = jnp.floor(rank * (1.0 / RET))
    ret = b_row * RET + (rank - turn * RET) + turn * BACK
    ret_ref[...] = jnp.broadcast_to(ret, (8, LEAVES)).astype(I32)
    rounds = jnp.max(turn) + 1.0
    lane = iota((LEAVES, LANES), 1)
    extra = jnp.where(lane == 0, b_col + 1.0, jnp.where(lane == 1, rounds, 0.0)).astype(BF16)
    moves[2].wait()
    for first in range(0, SLOTS, TILE):
        hot = onehot_rows(first, TILE, slot)
        out_ref[first : first + TILE, :D] = dot(hot, leaves_ref[...]).astype(BF16)
        out_ref[first : first + TILE, D:] = dot(hot, extra).astype(BF16)


def tags_of(x_ref):
    tags = x_ref[:, D:]
    picks = jnp.where(iota((8, LANES), 0) == iota((8, LANES), 1), 1.0, 0.0).astype(BF16)
    rows = dot_nt(picks, tags)
    spread = jnp.where(iota((LANES, LANES), 0) == 0, 1.0, 0.0).astype(BF16)
    return rows[0:1, :], dot(tags, spread), jnp.max(rows[1:2, :])


def ranks_of(tag_row, tag_col):
    ranks = []
    for part in range(tag_row.shape[1] // LANES):
        row = tag_row[:, part * LANES : (part + 1) * LANES]
        block = tag_col[part * LANES : (part + 1) * LANES, :]
        before = iota((LANES, LANES), 0) < iota((LANES, LANES), 1)
        hits = jnp.where(before, jnp.where(block == row, 1.0, 0.0), 0.0)
        rank = jnp.sum(hits, axis=0, keepdims=True)
        if part:
            above = jnp.where(tag_col[: part * LANES, :] == row, 1.0, 0.0)
            rank = rank + jnp.sum(above, axis=0, keepdims=True)
        ranks.append(rank)
    return jnp.concatenate(ranks, axis=1)


def rms(values, gain):
    mean_sq = jnp.mean(values * values, axis=-1, keepdims=True)
    return (values * lax.rsqrt(mean_sq + EPSILON) * gain).astype(BF16)


def fetch(layer_index, sources, targets, sems):
    moves = []
    for index, (source, target) in enumerate(zip(sources, targets)):
        part = source if index >= 6 else source.at[layer_index]
        moves.append(pltpu.make_async_copy(part, target, sems.at[index]))
        moves[-1].start()
    return moves


def layer(layer_index, count, tile, x_ref, tag_row, weights, y_ref, q_ref, k_ref, v_ref):
    wq, wk, wv, wo, wu, wd, gain_one, gain_two = weights
    one = gain_one[layer_index : layer_index + 1, :]
    two = gain_two[layer_index : layer_index + 1, :]
    head_of = iota((tile, D), 1) // HEAD_DIM

    def project(step, _):
        rows = pl.ds(pl.multiple_of(step * tile, tile), tile)
        normed = rms(x_ref[rows, :D].astype(F32), one)
        q_ref[rows, :] = dot(normed, wq[...]).astype(BF16) * jnp.asarray(HEAD_DIM**-0.5, BF16)
        k_ref[rows, :] = dot(normed, wk[...]).astype(BF16)
        value = dot(normed, wv[...]).astype(BF16)
        for head in range(HEADS):
            v_ref[head, rows, :] = jnp.where(head_of == head, value, jnp.asarray(1, BF16))
        return 0

    lax.fori_loop(0, count // tile, project, 0)
    live = tag_row > 0.0

    def attend(step, _):
        rows = pl.ds(pl.multiple_of(step * tile, tile), tile)
        query = q_ref[rows, :]
        top = jnp.zeros((tile, D), F32)
        total = jnp.zeros((tile, D), F32)
        for head in range(HEADS):
            own = jnp.where(head_of == head, query, jnp.asarray(0, BF16))
            scores = dot_nt(own, k_ref[:count, :])
            scores = jnp.where(live, scores, NEGATIVE)
            peak = jnp.max(scores, axis=-1, keepdims=True)
            probs = jnp.exp2((scores - peak) * LOG2E).astype(BF16)
            mixed = dot(probs, v_ref[head, :count, :])
            top = jnp.where(head_of == head, mixed, top)
            total = jnp.where(head_of == (head + 1) % HEADS, mixed, total)
        total = pltpu.roll(total, D - HEAD_DIM, 1)
        att = (top / total).astype(BF16)
        hidden = x_ref[rows, :D].astype(F32) + dot(att, wo[...])
        up = jax.nn.gelu(dot(rms(hidden, two), wu[...])).astype(BF16)
        y_ref[rows, :] = (hidden + dot(up, wd[...])).astype(BF16)
        return 0

    lax.fori_loop(0, count // tile, attend, 0)


def layer_a_kernel(x_ref, *refs):
    sources, out_ref, weights, sems, (y_ref, q_ref, k_ref, v_ref) = refs[:8], refs[8], refs[9:17], refs[17], refs[18:]
    moves = fetch(0, sources, weights, sems)
    tag_row, tag_col, rounds = tags_of(x_ref)
    slot = (tag_row - 1.0) * CAP + ranks_of(tag_row, tag_col)
    slot = jnp.where(tag_row > 0.0, slot, -1.0).astype(I32)
    lane = iota((SLOTS, LANES), 1)
    home = iota((SLOTS, LANES), 0) // CAP + 1
    extra = jnp.where(lane == 0, home.astype(F32), 0.0).astype(BF16)
    for move in moves:
        move.wait()
    layer(0, SLOTS, TILE, x_ref, tag_row, weights, y_ref, q_ref, k_ref, v_ref)
    for first in range(0, SLOTS, TILE):
        hot = onehot_rows(first, TILE, slot)
        out_ref[first : first + TILE, :D] = dot(hot, y_ref[...]).astype(BF16)
        tail = jnp.where(lane[:TILE] == 1, rounds, dot(hot, extra))
        out_ref[first : first + TILE, D:] = tail.astype(BF16)


def finish_b(count, tile, x_ref, tag_row, tag_col, weights, refs):
    out_ref, y_ref, slot_ref, q_ref, k_ref, v_ref = refs
    layer(1, count, tile, x_ref, tag_row, weights, y_ref, q_ref, k_ref, v_ref)
    rank = ranks_of(tag_row, tag_col)
    turn = jnp.floor(rank * (1.0 / RET))
    slot = (tag_row - 1.0) * RET + (rank - turn * RET) + turn * BACK
    slot = jnp.where(tag_row > 0.0, slot, -1.0).astype(I32)
    slot_ref[:, :count] = jnp.broadcast_to(slot, (8, count))
    for first in range(0, BACK, TILE):
        hot = onehot_rows(first, TILE, slot)
        out_ref[first : first + TILE, :] = dot(hot, y_ref[:count, :]).astype(BF16)


def before(flags):
    parts = flags.shape[1] // LANES
    square = jnp.concatenate([flags[:, p * LANES : (p + 1) * LANES] for p in range(parts)], axis=0)
    upper = jnp.where(iota((LANES, LANES), 0) < iota((LANES, LANES), 1), 1.0, 0.0).astype(BF16)
    inner = dot(square.astype(BF16), upper)
    held = jnp.zeros((1, 1), F32)
    rows = []
    for p in range(parts):
        rows.append(inner[p : p + 1, :] + held)
        held = held + jnp.sum(square[p : p + 1, :], axis=1, keepdims=True)
    return jnp.concatenate(rows, axis=1)


def layer_b_kernel(x_ref, *refs):
    sources, (out_ref, y_ref, slot_ref, rounds_ref) = refs[:8], refs[8:12]
    weights, sems, (q_ref, k_ref, v_ref, packed_ref) = refs[12:20], refs[20], refs[21:]
    moves = fetch(1, sources, weights, sems)
    tag_row, tag_col, rounds = tags_of(x_ref)
    rounds_ref[0] = rounds.astype(I32)
    rest = (out_ref, y_ref, slot_ref, q_ref, k_ref, v_ref)
    live = jnp.where(tag_row > 0.0, 1.0, 0.0)
    total = jnp.sum(live)

    @pl.when(total <= FEW)
    def _():
        place = jnp.where(tag_row > 0.0, before(live), -1.0).astype(I32)
        for first in range(0, FEW, LANES):
            hot = onehot_rows(first, LANES, place)
            packed_ref[first : first + LANES, :] = dot(hot, x_ref[...]).astype(BF16)
        few_row, few_col, _ = tags_of(packed_ref)
        slot_ref[:, FEW:] = jnp.full((8, SLOTS - FEW), -1, I32)
        y_ref[FEW:, :] = jnp.zeros((SLOTS - FEW, D), BF16)
        for move in moves:
            move.wait()
        finish_b(FEW, FEW // 2, packed_ref, few_row, few_col, weights, rest)

    @pl.when(total > FEW)
    def _():
        for move in moves:
            move.wait()
        finish_b(SLOTS, TILE, x_ref, tag_row, tag_col, weights, rest)


def call_layer(kernel, out_shape, x, weights):
    kernel_weights = [pltpu.VMEM(weight.shape[1:], BF16) for weight in weights[:6]]
    kernel_weights += [pltpu.VMEM(gain.shape, F32) for gain in weights[6:]]
    scratch = [
        pltpu.VMEM((SLOTS, D), BF16),
        pltpu.VMEM((SLOTS, D), BF16),
        pltpu.VMEM((HEADS, SLOTS, D), BF16),
    ]
    if len(out_shape) == 1:
        scratch = [pltpu.VMEM((SLOTS, D), BF16)] + scratch
    else:
        scratch = scratch + [pltpu.VMEM((FEW, WIDE), BF16)]
    return pl.pallas_call(
        kernel,
        out_shape=out_shape,
        in_specs=[VMEM] + [pl.BlockSpec(memory_space=pltpu.HBM)] * 8,
        out_specs=[pl.BlockSpec(memory_space=pltpu.SMEM if shape.shape == (1,) else pltpu.VMEM) for shape in out_shape],
        scratch_shapes=kernel_weights + [pltpu.SemaphoreType.DMA((8,))] + scratch,
        compiler_params=pltpu.CompilerParams(vmem_limit_bytes=24 * 2**20),
        cost_estimate=pl.CostEstimate(flops=6 * 10**9, bytes_accessed=4 * 2**20, transcendentals=5 * 2**20),
    )(x, *map(kept, weights))


def resend_kernel(turn_ref, y_ref, slot_ref, out_ref):
    slot = slot_ref[0:1, :] - turn_ref[0] * BACK
    for first in range(0, BACK, TILE):
        hot = onehot_rows(first, TILE, slot)
        out_ref[first : first + TILE, :] = dot(hot, y_ref[...]).astype(BF16)


def gathered(want, back_ref):
    parts = []
    for first in range(0, LEAVES, LANES):
        block = want[first : first + LANES, :]
        hot = jnp.concatenate(
            [
                jnp.where(block == iota((LANES, LANES), 1) + lanes, 1.0, 0.0).astype(BF16)
                for lanes in range(0, BACK, LANES)
            ],
            axis=1,
        )
        parts.append(dot(hot, back_ref[...]))
    return jnp.concatenate(parts, axis=0)


def regather_kernel(turn_ref, back_ref, want_ref, held_ref, out_ref):
    rows = gathered(want_ref[...] - turn_ref[0] * BACK, back_ref)
    out_ref[...] = (held_ref[...].astype(F32) + rows).astype(BF16)


def order_kernel(ret_ref, parent_ref, want_ref, block_ref, start_ref):
    parent = parent_ref[...].astype(F32)
    ret = ret_ref[0:1, :].astype(F32)
    p_col = columns(parent, LEAVES)
    l_col = fiota((LEAVES, LANES), 0)
    parts = []
    for part in range(LEAVES // LANES):
        pr = parent[:, part * LANES : (part + 1) * LANES]
        lr = fiota((1, LANES), 1) + part * LANES
        less = jnp.where(p_col * LEAVES + l_col < pr * LEAVES + lr, 1.0, 0.0)
        parts.append(jnp.sum(less, axis=0, keepdims=True))
    place = jnp.concatenate(parts, axis=1)
    for first in range(0, LEAVES, LANES):
        rows = slice(first, first + LANES)
        hit = place == fiota((LANES, LEAVES), 0) + first
        want = jnp.sum(jnp.where(hit, ret, 0.0), axis=1, keepdims=True)
        want_ref[rows, :] = jnp.broadcast_to(want, (LANES, LANES)).astype(I32)
        block = 2.0 * jnp.sum(jnp.where(hit, parent, 0.0), axis=1, keepdims=True)
        block_ref[rows, :] = jnp.broadcast_to(block, (LANES, LANES))
    block_ref[LEAVES:, :] = jnp.full((GROUP, LANES), -8.0, F32)
    below = jnp.where(p_col < fiota((1, LANES), 1) * LANES, 1.0, 0.0)
    start_ref[...] = jnp.broadcast_to(jnp.sum(below, axis=0, keepdims=True), (8, LANES)).astype(I32)


def call_order(ret, parent):
    return pl.pallas_call(
        order_kernel,
        out_shape=[
            jax.ShapeDtypeStruct((LEAVES, LANES), I32),
            jax.ShapeDtypeStruct((LEAVES + GROUP, LANES), F32),
            jax.ShapeDtypeStruct((8, LANES), I32),
        ],
        in_specs=[VMEM, VMEM],
        out_specs=[VMEM, VMEM, VMEM],
        compiler_params=pltpu.CompilerParams(vmem_limit_bytes=24 * 2**20),
        cost_estimate=pl.CostEstimate(flops=10**9, bytes_accessed=2**20, transcendentals=0),
    )(ret, parent)


STRIP = 8


def conv_kernel(count, main_ref, above_ref, below_ref, head_ref, foot_ref, weight_ref, out_ref, w_ref):
    step = pl.program_id(0)

    @pl.when(step == 0)
    def _():
        zero = jnp.zeros((LANES, LANES), BF16)
        for b in range(3):
            for row in range(4):
                for r in range(2):
                    block = weight_ref[row - r, b] if 0 <= row - r < 3 else zero
                    w_ref[b, row * LANES : (row + 1) * LANES, r * LANES : (r + 1) * LANES] = block

    above = jnp.where(step == 0, head_ref[0, 0], above_ref[0, 0])
    below = jnp.where(step == count - 1, foot_ref[0, 0], below_ref[0, 0])
    rows = [above] + [main_ref[0, r] for r in range(STRIP)] + [below]
    column = iota((TILE, TILE), 0)
    for pair in range(STRIP // 2):
        wide = jnp.concatenate(rows[2 * pair : 2 * pair + 4], axis=1)
        left = pltpu.roll(dot(wide, w_ref[0]), 1, 0)
        right = pltpu.roll(dot(wide, w_ref[2]), TILE - 1, 0)
        both = dot(wide, w_ref[1])
        both = both + jnp.where(column == 0, 0.0, left) + jnp.where(column == TILE - 1, 0.0, right)
        out_ref[0, 2 * pair] = both[:, :LANES].astype(BF16)
        out_ref[0, 2 * pair + 1] = both[:, LANES:].astype(BF16)


def call_conv(coarse, head, foot, weight):
    rows, cols, channels = coarse.shape[1:]
    count = rows // STRIP
    single = (1, 1, cols, channels)
    return pl.pallas_call(
        functools.partial(conv_kernel, count),
        grid=(count,),
        out_shape=jax.ShapeDtypeStruct(coarse.shape, BF16),
        in_specs=[
            pl.BlockSpec((1, STRIP, cols, channels), lambda i: (0, i, 0, 0)),
            pl.BlockSpec(single, lambda i: (0, jnp.maximum(i * STRIP - 1, 0), 0, 0)),
            pl.BlockSpec(single, lambda i: (0, jnp.minimum(i * STRIP + STRIP, rows - 1), 0, 0)),
            pl.BlockSpec(single, lambda i: (0, 0, 0, 0)),
            pl.BlockSpec(single, lambda i: (0, 0, 0, 0)),
            pl.BlockSpec(weight.shape, lambda i: (0, 0, 0, 0)),
        ],
        out_specs=pl.BlockSpec((1, STRIP, cols, channels), lambda i: (0, i, 0, 0)),
        scratch_shapes=[pltpu.VMEM((3, 4 * LANES, 2 * LANES), BF16)],
        compiler_params=pltpu.CompilerParams(vmem_limit_bytes=24 * 2**20),
        cost_estimate=pl.CostEstimate(flops=6 * 10**9, bytes_accessed=8 * 2**20, transcendentals=0),
    )(*[kept(coarse)] * 3, head, foot, weight)


def field_kernel(start_ref, conv_ref, back_ref, held_ref, want_ref, block_ref, we_ref, wp_ref, out_ref, pix_ref):
    step = pl.program_id(0)

    @pl.when(step == 0)
    def _():
        leaf = (gathered(want_ref[...], back_ref) + held_ref[...].astype(F32)).astype(BF16)
        expanded = jax.nn.gelu(dot(leaf, we_ref[...])).astype(BF16)
        pixels = dot(expanded, wp_ref[...]).astype(BF16)
        for c in range(2):
            for r in range(2):
                lanes = slice(r * LANES, (r + 1) * LANES)
                pix_ref[c, :LEAVES, lanes] = pixels[:, (2 * r + c) * LANES : (2 * r + c + 1) * LANES]
            pix_ref[c, LEAVES:, :] = jnp.zeros((GROUP, D), BF16)

    def added(index, first):
        rows = pl.ds(pl.multiple_of(first, ALIGN), GROUP)
        spots = block_ref[rows, :].T[0:1, :] - (index * TILE).astype(F32)
        spots = jnp.concatenate([spots, spots + 1.0], axis=1).astype(I32)
        hot = jnp.where(iota((TILE, 2 * GROUP), 0) == spots, 1.0, 0.0).astype(BF16)
        return dot(hot, jnp.concatenate([pix_ref[0, rows, :], pix_ref[1, rows, :]], axis=0))

    def held_rows(pair):
        return jnp.concatenate([conv_ref[0, 2 * pair], conv_ref[0, 2 * pair + 1]], axis=1).astype(F32)

    def store(pair, total):
        out_ref[0, 2 * pair] = total[:, :LANES].astype(BF16)
        out_ref[0, 2 * pair + 1] = total[:, LANES:].astype(BF16)

    pairs = []
    for pair in range(STRIP // 2):
        index = step * (STRIP // 2) + pair
        first = start_ref[index] // ALIGN * ALIGN
        pairs.append((pair, index, first, start_ref[index + 1]))
        store(pair, held_rows(pair) + added(index, first))
    for pair, index, first, end in pairs:

        @pl.when(end > first + GROUP)
        def _():
            more = lambda part, total: total + added(index, first + part * GROUP)
            store(pair, lax.fori_loop(0, (end - first + GROUP - 1) // GROUP, more, held_rows(pair)))


def call_field(starts, conv, back, held, want, block, w_expand, w_pixels):
    rows, cols, channels = conv.shape[1:]
    whole = lambda *shape: pl.BlockSpec(shape, lambda i, s: (0,) * len(shape))
    strip = pl.BlockSpec((1, STRIP, cols, channels), lambda i, s: (0, i, 0, 0))
    return pl.pallas_call(
        field_kernel,
        grid_spec=pltpu.PrefetchScalarGridSpec(
            num_scalar_prefetch=1,
            grid=(rows // STRIP,),
            in_specs=[
                strip,
                whole(BACK, D),
                whole(LEAVES, D),
                whole(LEAVES, LANES),
                whole(LEAVES + GROUP, LANES),
                whole(D, D),
                whole(D, 4 * LANES),
            ],
            out_specs=strip,
            scratch_shapes=[pltpu.VMEM((2, LEAVES + GROUP, D), BF16)],
        ),
        out_shape=jax.ShapeDtypeStruct(conv.shape, BF16),
        compiler_params=pltpu.CompilerParams(vmem_limit_bytes=32 * 2**20),
        cost_estimate=pl.CostEstimate(flops=2 * 10**9, bytes_accessed=10 * 2**20, transcendentals=2**17),
    )(starts, kept(conv), back, held, want, block, w_expand, w_pixels)


def exchange(rows, capacity):
    width = rows.shape[1]
    blocks = rows.reshape(DEVICES, capacity, width)
    moved = lax.all_to_all(blocks, ("tile", "intra"), split_axis=0, concat_axis=0, tiled=True)
    return moved.reshape(DEVICES * capacity, width)


def shards(
    leaves,
    window_a,
    window_b,
    parent,
    coarse,
    w_query,
    w_key,
    w_value,
    w_out,
    w_up,
    w_down,
    gain_attn,
    gain_mlp,
    w_expand,
    w_pixels,
    conv_weight,
):
    weights = (w_query, w_key, w_value, w_out, w_up, w_down, gain_attn, gain_mlp)
    count = lax.axis_size("intra")
    rows = coarse.shape[1]
    head = lax.ppermute(coarse[:, rows - 1 :], "intra", [(i, i + 1) for i in range(count - 1)])
    foot = lax.ppermute(coarse[:, :1], "intra", [(i + 1, i) for i in range(count - 1)])
    sent, ret = pl.pallas_call(
        send_kernel,
        out_shape=[jax.ShapeDtypeStruct((SLOTS, WIDE), BF16), jax.ShapeDtypeStruct((8, LEAVES), I32)],
        in_specs=[pl.BlockSpec(memory_space=pltpu.HBM)] * 3,
        out_specs=[VMEM] * 2,
        scratch_shapes=[
            pltpu.VMEM((LEAVES, D), BF16),
            pltpu.VMEM((1, LEAVES), I32),
            pltpu.VMEM((1, LEAVES), I32),
            pltpu.SemaphoreType.DMA((3,)),
        ],
        compiler_params=pltpu.CompilerParams(vmem_limit_bytes=24 * 2**20),
        cost_estimate=pl.CostEstimate(flops=10**9, bytes_accessed=2**20, transcendentals=0),
    )(*map(kept, (leaves, window_a.reshape(1, LEAVES), window_b.reshape(1, LEAVES))))
    rows_a = exchange(sent, CAP)
    want, block, starts = call_order(ret, parent.reshape(1, LEAVES))
    rows_a, want, head, foot = lax.optimization_barrier((rows_a, want, head, foot))
    (sent_b,) = call_layer(
        layer_a_kernel, [jax.ShapeDtypeStruct((SLOTS, WIDE), BF16)], rows_a, weights
    )
    rows_b = exchange(sent_b, CAP)
    conv = call_conv(coarse, head, foot, conv_weight)
    rows_b, conv = lax.optimization_barrier((rows_b, conv))
    home, y, slot, rounds = call_layer(
        layer_b_kernel,
        [
            jax.ShapeDtypeStruct((BACK, D), BF16),
            jax.ShapeDtypeStruct((SLOTS, D), BF16),
            jax.ShapeDtypeStruct((8, SLOTS), I32),
            jax.ShapeDtypeStruct((1,), I32),
        ],
        rows_b,
        weights,
    )
    back = exchange(home, RET)
    total = rounds.reshape(())

    def more(state):
        return state[0] < total

    def again(state):
        turn, held = state
        index = turn.reshape(1)
        smem = pl.BlockSpec(memory_space=pltpu.SMEM)
        part = pl.pallas_call(
            resend_kernel,
            out_shape=jax.ShapeDtypeStruct((BACK, D), BF16),
            in_specs=[smem, VMEM, VMEM],
            out_specs=VMEM,
        )(index, y, slot)
        held = pl.pallas_call(
            regather_kernel,
            out_shape=jax.ShapeDtypeStruct((LEAVES, D), BF16),
            in_specs=[smem, VMEM, VMEM, VMEM],
            out_specs=VMEM,
        )(index, exchange(part, RET), want, held)
        return turn + 1, held

    _, held = lax.while_loop(more, again, (jnp.asarray(1, I32), jnp.zeros((LEAVES, D), BF16)))
    return call_field(starts[0], conv, back, held, want, block, w_expand, w_pixels)


def solution(mesh):
    placed = (
        P(("tile", "intra"), None),
        P(("tile", "intra")),
        P(("tile", "intra")),
        P(("tile", "intra")),
        P("tile", "intra", None, None),
    ) + (P(),) * 11
    return jax.shard_map(
        shards,
        mesh=mesh,
        in_specs=placed,
        out_specs=P("tile", "intra", None, None),
        check_vma=False,
    )
```

```python
import functools
import math

import jax
import jax.numpy as jnp
from jax import lax
from jax.experimental import pallas as pl
from jax.experimental.pallas import tpu as pltpu
from jax.sharding import PartitionSpec as P

HEADS = 4
HEAD_DIM = 64
EPSILON = 1e-06
NEGATIVE = -1e30
LOG2E = math.log2(math.e)
GELU = math.sqrt(2.0 / math.pi)
D = 256
LANES = 128
WIDE = D + LANES
DEVICES = 128
CAP = 8
SLOTS = DEVICES * CAP
LEAVES = 512
RET = 16
BACK = DEVICES * RET
FEW = 640
GROUP = 64
ALIGN = 16
SPAN = 1024
BAND = 16
TILE = 256
FF = 1024
F32 = jnp.float32
BF16 = jnp.bfloat16
I32 = jnp.int32

VMEM = pl.BlockSpec(memory_space=pltpu.VMEM)


def kept(array):
    return pltpu.with_memory_space_constraint(array, pltpu.HBM)


def iota(shape, dim):
    return lax.broadcasted_iota(I32, shape, dim)


def fiota(shape, dim):
    return iota(shape, dim).astype(F32)


def dot(a, b):
    return jnp.dot(a, b, preferred_element_type=F32)


def dot_nt(a, b):
    return lax.dot_general(a, b, (((1,), (1,)), ((), ())), preferred_element_type=F32)


def columns(row, count):
    return jnp.broadcast_to(row, (LANES, count)).T


def onehot_rows(first, rows, targets):
    want = iota((rows, targets.shape[1]), 0) + first
    return jnp.where(want == targets, 1.0, 0.0).astype(BF16)


def send_kernel(leaves_hbm, wa_hbm, wb_hbm, out_ref, ret_ref, leaves_ref, wa_ref, wb_ref, sems):
    moves = [
        pltpu.make_async_copy(source, target, sems.at[index])
        for index, (source, target) in enumerate(((wa_hbm, wa_ref), (wb_hbm, wb_ref), (leaves_hbm, leaves_ref)))
    ]
    for move in moves:
        move.start()
    moves[0].wait()
    moves[1].wait()
    a_row = wa_ref[...].astype(F32)
    b_row = wb_ref[...].astype(F32)
    a_col = columns(a_row, LEAVES)
    b_col = columns(b_row, LEAVES)
    l_col = fiota((LEAVES, LANES), 0)
    key_col = a_col * LEAVES + l_col
    slots = []
    ranks = []
    for part in range(LEAVES // LANES):
        lanes = slice(part * LANES, (part + 1) * LANES)
        ar = a_row[:, lanes]
        br = b_row[:, lanes]
        lr = fiota((1, LANES), 1) + part * LANES
        same_a = jnp.where(a_col == ar, jnp.where(l_col < lr, 1.0, 0.0), 0.0)
        same_b = jnp.where(b_col == br, jnp.where(key_col < ar * LEAVES + lr, 1.0, 0.0), 0.0)
        slots.append(ar * CAP + jnp.sum(same_a, axis=0, keepdims=True))
        ranks.append(jnp.sum(same_b, axis=0, keepdims=True))
    slot = jnp.concatenate(slots, axis=1).astype(I32)
    rank = jnp.concatenate(ranks, axis=1)
    turn = jnp.floor(rank * (1.0 / RET))
    ret = b_row * RET + (rank - turn * RET) + turn * BACK
    ret_ref[...] = jnp.broadcast_to(ret, (8, LEAVES)).astype(I32)
    rounds = jnp.max(turn) + 1.0
    lane = iota((LEAVES, LANES), 1)
    extra = jnp.where(lane == 0, b_col + 1.0, jnp.where(lane == 1, rounds, 0.0)).astype(BF16)
    moves[2].wait()
    for first in range(0, SLOTS, SPAN):
        hot = onehot_rows(first, SPAN, slot)
        out_ref[first : first + SPAN, :D] = dot(hot, leaves_ref[...]).astype(BF16)
        out_ref[first : first + SPAN, D:] = dot(hot, extra).astype(BF16)


def tags_of(x_ref):
    tags = x_ref[:, D:]
    picks = jnp.where(iota((8, LANES), 0) == iota((8, LANES), 1), 1.0, 0.0).astype(BF16)
    rows = dot_nt(picks, tags)
    spread = jnp.where(iota((LANES, LANES), 0) == 0, 1.0, 0.0).astype(BF16)
    return rows[0:1, :], dot(tags, spread), jnp.max(rows[1:2, :])


def ranks_of(tag_row, tag_col):
    ranks = []
    for part in range(tag_row.shape[1] // LANES):
        row = tag_row[:, part * LANES : (part + 1) * LANES]
        block = tag_col[part * LANES : (part + 1) * LANES, :]
        before = iota((LANES, LANES), 0) < iota((LANES, LANES), 1)
        hits = jnp.where(before, jnp.where(block == row, 1.0, 0.0), 0.0)
        rank = jnp.sum(hits, axis=0, keepdims=True)
        if part:
            above = jnp.where(tag_col[: part * LANES, :] == row, 1.0, 0.0)
            rank = rank + jnp.sum(above, axis=0, keepdims=True)
        ranks.append(rank)
    return jnp.concatenate(ranks, axis=1)


def rms(values, gain):
    mean_sq = jnp.mean(values * values, axis=-1, keepdims=True)
    return (values * lax.rsqrt(mean_sq + EPSILON) * gain).astype(BF16)


def fetch(layer_index, sources, targets, sems):
    moves = []
    for index, (source, target) in enumerate(zip(sources, targets)):
        part = source if index >= 6 else source.at[layer_index]
        moves.append(pltpu.make_async_copy(part, target, sems.at[index]))
        moves[-1].start()
    return moves


def gelu_twice(x):
    inner = x * (x * x * (0.044715 * GELU) + GELU)
    return x + x * jnp.tanh(inner)


def layer(layer_index, count, tile, x_ref, live, weights, y_ref, q_ref, k_ref, v_ref, live_ref):
    wq, wk, wv, wo, wu, wd, gain_one, gain_two = weights
    one = gain_one[layer_index : layer_index + 1, :]
    two = gain_two[layer_index : layer_index + 1, :]
    low = iota((tile, LANES), 1) < HEAD_DIM
    zero = jnp.asarray(0, BF16)
    live_ref[:count, :] = live.astype(BF16)
    first = dot(rms(x_ref[:ALIGN, :D].astype(F32), one), wk[...])[0:1, :].astype(BF16)

    def project(step, _):
        rows = pl.ds(pl.multiple_of(step * tile, tile), tile)
        normed = rms(x_ref[rows, :D].astype(F32), one)
        flag = live_ref[rows, :]
        q_ref[rows, :] = (dot(normed, wq[...]) * (HEAD_DIM**-0.5 * LOG2E)).astype(BF16)
        key = dot(normed, wk[...]).astype(BF16)
        k_ref[rows, :] = jnp.where(jnp.concatenate([flag, flag], axis=1) > 0, key, first)
        value = dot(normed, wv[...]).astype(BF16)
        for pair in range(HEADS // 2):
            part = value[:, pair * LANES : (pair + 1) * LANES]
            lanes = slice(pair * LANES, (pair + 1) * LANES)
            v_ref[2 * pair, rows, lanes] = jnp.where(low, part, flag)
            v_ref[2 * pair + 1, rows, lanes] = jnp.where(low, flag, part)
            other = slice((1 - pair) * LANES, (2 - pair) * LANES)
            v_ref[2 * pair, rows, other] = flag
            v_ref[2 * pair + 1, rows, other] = flag
        return 0

    lax.fori_loop(0, count // tile, project, 0)

    def attend(step, _):
        rows = pl.ds(pl.multiple_of(step * tile, tile), tile)

        def scored(head):
            lanes = slice(head // 2 * LANES, (head // 2 + 1) * LANES)
            query = q_ref[rows, lanes]
            own = jnp.where(low, query, zero) if head % 2 == 0 else jnp.where(low, zero, query)
            return dot_nt(own, k_ref[:count, lanes])

        def mixed(head, scores):
            peak = jnp.max(scores, axis=-1, keepdims=True)
            lanes = slice(head // 2 * LANES, (head // 2 + 1) * LANES)
            return dot(jnp.exp2(scores - peak).astype(BF16), v_ref[head, :count, :])[:, lanes]

        ahead = scored(0)
        outs = []
        for head in range(HEADS):
            scores = ahead
            if head + 1 < HEADS:
                ahead = scored(head + 1)
            outs.append(mixed(head, scores))
        parts = []
        for pair in range(HEADS // 2):
            even, odd = outs[2 * pair : 2 * pair + 2]
            total = pltpu.roll(jnp.where(low, odd, even), HEAD_DIM, 1)
            parts.append(jnp.where(low, even, odd) / total)
        att = jnp.concatenate(parts, axis=1).astype(BF16)
        hidden = x_ref[rows, :D].astype(F32) + dot(att, wo[...])
        up = gelu_twice(dot(rms(hidden, two), wu[...])).astype(BF16)
        y_ref[rows, :] = (hidden + 0.5 * dot(up, wd[...])).astype(BF16)
        return 0

    lax.fori_loop(0, count // tile, attend, 0)


def layer_a_kernel(x_ref, *refs):
    sources, out_ref, weights, sems, (y_ref, *rest) = refs[:8], refs[8], refs[9:17], refs[17], refs[18:]
    moves = fetch(0, sources, weights, sems)
    tag_row, tag_col, rounds = tags_of(x_ref)
    slot = (tag_row - 1.0) * CAP + ranks_of(tag_row, tag_col)
    slot = jnp.where(tag_row > 0.0, slot, -1.0).astype(I32)
    lane = iota((SLOTS, LANES), 1)
    home = iota((SLOTS, LANES), 0) // CAP + 1
    extra = jnp.where(lane == 0, home.astype(F32), 0.0).astype(BF16)
    for move in moves:
        move.wait()
    live = jnp.where(tag_col > 0.0, 1.0, 0.0)
    layer(0, SLOTS, 2 * TILE, x_ref, live, weights, y_ref, *rest)
    for first in range(0, SLOTS, SPAN):
        hot = onehot_rows(first, SPAN, slot)
        out_ref[first : first + SPAN, :D] = dot(hot, y_ref[...]).astype(BF16)
        tail = jnp.where(lane[:SPAN] == 1, rounds, dot(hot, extra))
        out_ref[first : first + SPAN, D:] = tail.astype(BF16)


def finish_b(count, tile, place, x_ref, packed_ref, weights, moves, refs):
    out_ref, y_ref, slot_ref, *rest = refs
    packed_ref[:count, :] = dot(onehot_rows(0, count, place), x_ref[...]).astype(BF16)
    tag_row, tag_col, _ = tags_of(packed_ref.at[:count, :])
    rank = ranks_of(tag_row, tag_col)
    turn = jnp.floor(rank * (1.0 / RET))
    slot = (tag_row - 1.0) * RET + (rank - turn * RET) + turn * BACK
    slot = jnp.where(tag_row > 0.0, slot, -1.0).astype(I32)
    slot_ref[:, :count] = jnp.broadcast_to(slot, (8, count))
    if count < SLOTS:
        slot_ref[:, count:] = jnp.full((8, SLOTS - count), -1, I32)
        y_ref[count:, :] = jnp.zeros((SLOTS - count, D), BF16)
    live = jnp.where(iota((count, LANES), 0) == 0, 1.0, jnp.where(tag_col > 0.0, 1.0, 0.0))
    for move in moves:
        move.wait()
    layer(1, count, tile, packed_ref, live, weights, y_ref, *rest)
    for first in range(0, BACK, SPAN):
        hot = onehot_rows(first, SPAN, slot)
        out_ref[first : first + SPAN, :] = dot(hot, y_ref[:count, :]).astype(BF16)


def before(flags):
    parts = flags.shape[1] // LANES
    square = jnp.concatenate([flags[:, p * LANES : (p + 1) * LANES] for p in range(parts)], axis=0)
    upper = jnp.where(iota((LANES, LANES), 0) < iota((LANES, LANES), 1), 1.0, 0.0).astype(BF16)
    inner = dot(square.astype(BF16), upper)
    held = jnp.zeros((1, 1), F32)
    rows = []
    for p in range(parts):
        rows.append(inner[p : p + 1, :] + held)
        held = held + jnp.sum(square[p : p + 1, :], axis=1, keepdims=True)
    return jnp.concatenate(rows, axis=1)


def layer_b_kernel(x_ref, *refs):
    sources, (out_ref, y_ref, slot_ref, rounds_ref) = refs[:8], refs[8:12]
    weights, sems, (packed_ref, *rest) = refs[12:20], refs[20], refs[21:]
    moves = fetch(1, sources, weights, sems)
    tag_row, _, rounds = tags_of(x_ref)
    rounds_ref[0] = rounds.astype(I32)
    live = jnp.where(tag_row > 0.0, 1.0, 0.0)
    total = jnp.sum(live)
    place = jnp.where(tag_row > 0.0, before(live), -1.0).astype(I32)
    outs = (out_ref, y_ref, slot_ref, *rest)

    @pl.when(total <= FEW)
    def _():
        finish_b(FEW, FEW // 2, place, x_ref, packed_ref, weights, moves, outs)

    @pl.when(total > FEW)
    def _():
        finish_b(SLOTS, TILE, place, x_ref, packed_ref, weights, moves, outs)


def call_layer(kernel, out_shape, x, weights):
    kernel_weights = [pltpu.VMEM(weight.shape[1:], BF16) for weight in weights[:6]]
    kernel_weights += [pltpu.VMEM(gain.shape, F32) for gain in weights[6:]]
    scratch = [
        pltpu.VMEM((SLOTS, D) if len(out_shape) == 1 else (SLOTS, WIDE), BF16),
        pltpu.VMEM((SLOTS, D), BF16),
        pltpu.VMEM((SLOTS, D), BF16),
        pltpu.VMEM((HEADS, SLOTS, D), BF16),
        pltpu.VMEM((SLOTS, LANES), BF16),
    ]
    return pl.pallas_call(
        kernel,
        out_shape=out_shape,
        in_specs=[VMEM] + [pl.BlockSpec(memory_space=pltpu.HBM)] * 8,
        out_specs=[pl.BlockSpec(memory_space=pltpu.SMEM if shape.shape == (1,) else pltpu.VMEM) for shape in out_shape],
        scratch_shapes=kernel_weights + [pltpu.SemaphoreType.DMA((8,))] + scratch,
        compiler_params=pltpu.CompilerParams(vmem_limit_bytes=24 * 2**20),
        cost_estimate=pl.CostEstimate(flops=6 * 10**9, bytes_accessed=4 * 2**20, transcendentals=5 * 2**20),
    )(x, *map(kept, weights))


def resend_kernel(turn_ref, y_ref, slot_ref, out_ref):
    slot = slot_ref[0:1, :] - turn_ref[0] * BACK
    for first in range(0, BACK, TILE):
        hot = onehot_rows(first, TILE, slot)
        out_ref[first : first + TILE, :] = dot(hot, y_ref[...]).astype(BF16)


def gathered(want, back_ref):
    parts = []
    for first in range(0, LEAVES, LANES):
        block = want[first : first + LANES, :]
        hot = jnp.concatenate(
            [
                jnp.where(block == iota((LANES, LANES), 1) + lanes, 1.0, 0.0).astype(BF16)
                for lanes in range(0, BACK, LANES)
            ],
            axis=1,
        )
        parts.append(dot(hot, back_ref[...]))
    return jnp.concatenate(parts, axis=0)


def regather_kernel(turn_ref, back_ref, want_ref, held_ref, out_ref):
    rows = gathered(want_ref[...] - turn_ref[0] * BACK, back_ref)
    out_ref[...] = (held_ref[...].astype(F32) + rows).astype(BF16)


def order_kernel(ret_ref, parent_ref, want_ref, block_ref, start_ref):
    parent = parent_ref[...].astype(F32)
    ret = ret_ref[0:1, :].astype(F32)
    p_col = columns(parent, LEAVES)
    l_col = fiota((LEAVES, LANES), 0)
    parts = []
    for part in range(LEAVES // LANES):
        pr = parent[:, part * LANES : (part + 1) * LANES]
        lr = fiota((1, LANES), 1) + part * LANES
        less = jnp.where(p_col * LEAVES + l_col < pr * LEAVES + lr, 1.0, 0.0)
        parts.append(jnp.sum(less, axis=0, keepdims=True))
    place = jnp.concatenate(parts, axis=1)
    for first in range(0, LEAVES, LANES):
        rows = slice(first, first + LANES)
        hit = place == fiota((LANES, LEAVES), 0) + first
        want = jnp.sum(jnp.where(hit, ret, 0.0), axis=1, keepdims=True)
        want_ref[rows, :] = jnp.broadcast_to(want, (LANES, LANES)).astype(I32)
        block = 2.0 * jnp.sum(jnp.where(hit, parent, 0.0), axis=1, keepdims=True)
        block_ref[rows, :] = jnp.broadcast_to(block, (LANES, LANES))
    block_ref[LEAVES:, :] = jnp.full((GROUP, LANES), -8.0, F32)
    below = jnp.where(p_col < fiota((1, LANES), 1) * LANES, 1.0, 0.0)
    start_ref[...] = jnp.broadcast_to(jnp.sum(below, axis=0, keepdims=True), (8, LANES)).astype(I32)


def call_order(ret, parent):
    return pl.pallas_call(
        order_kernel,
        out_shape=[
            jax.ShapeDtypeStruct((LEAVES, LANES), I32),
            jax.ShapeDtypeStruct((LEAVES + GROUP, LANES), F32),
            jax.ShapeDtypeStruct((8, LANES), I32),
        ],
        in_specs=[VMEM, VMEM],
        out_specs=[VMEM, VMEM, VMEM],
        compiler_params=pltpu.CompilerParams(vmem_limit_bytes=24 * 2**20),
        cost_estimate=pl.CostEstimate(flops=10**9, bytes_accessed=2**20, transcendentals=0),
    )(ret, parent)


STRIP = 8


def conv_kernel(count, main_ref, above_ref, below_ref, head_ref, foot_ref, weight_ref, out_ref, w_ref):
    step = pl.program_id(0)

    @pl.when(step == 0)
    def _():
        zero = jnp.zeros((LANES, LANES), BF16)
        for b in range(3):
            for row in range(4):
                for r in range(2):
                    block = weight_ref[row - r, b] if 0 <= row - r < 3 else zero
                    w_ref[b, row * LANES : (row + 1) * LANES, r * LANES : (r + 1) * LANES] = block

    above = jnp.where(step == 0, head_ref[0, 0], above_ref[0, 0])
    below = jnp.where(step == count - 1, foot_ref[0, 0], below_ref[0, 0])
    rows = [above] + [main_ref[0, r] for r in range(STRIP)] + [below]
    column = iota((TILE, TILE), 0)
    for pair in range(STRIP // 2):
        wide = jnp.concatenate(rows[2 * pair : 2 * pair + 4], axis=1)
        left = pltpu.roll(dot(wide, w_ref[0]), 1, 0)
        right = pltpu.roll(dot(wide, w_ref[2]), TILE - 1, 0)
        both = dot(wide, w_ref[1])
        both = both + jnp.where(column == 0, 0.0, left) + jnp.where(column == TILE - 1, 0.0, right)
        out_ref[0, 2 * pair] = both[:, :LANES].astype(BF16)
        out_ref[0, 2 * pair + 1] = both[:, LANES:].astype(BF16)


def call_conv(coarse, head, foot, weight):
    rows, cols, channels = coarse.shape[1:]
    count = rows // STRIP
    single = (1, 1, cols, channels)
    return pl.pallas_call(
        functools.partial(conv_kernel, count),
        grid=(count,),
        out_shape=jax.ShapeDtypeStruct(coarse.shape, BF16),
        in_specs=[
            pl.BlockSpec((1, STRIP, cols, channels), lambda i: (0, i, 0, 0)),
            pl.BlockSpec(single, lambda i: (0, jnp.maximum(i * STRIP - 1, 0), 0, 0)),
            pl.BlockSpec(single, lambda i: (0, jnp.minimum(i * STRIP + STRIP, rows - 1), 0, 0)),
            pl.BlockSpec(single, lambda i: (0, 0, 0, 0)),
            pl.BlockSpec(single, lambda i: (0, 0, 0, 0)),
            pl.BlockSpec(weight.shape, lambda i: (0, 0, 0, 0)),
        ],
        out_specs=pl.BlockSpec((1, STRIP, cols, channels), lambda i: (0, i, 0, 0)),
        scratch_shapes=[pltpu.VMEM((3, 4 * LANES, 2 * LANES), BF16)],
        compiler_params=pltpu.CompilerParams(vmem_limit_bytes=24 * 2**20),
        cost_estimate=pl.CostEstimate(flops=6 * 10**9, bytes_accessed=8 * 2**20, transcendentals=0),
    )(*[kept(coarse)] * 3, head, foot, weight)


def field_kernel(start_ref, conv_hbm, back_ref, held_ref, want_ref, block_ref, we_ref, wp_ref, out_ref, pix_ref, conv_ref, sems):
    step = pl.program_id(0)

    def move(part):
        rows = pl.ds(part * BAND, BAND)
        return pltpu.make_async_copy(conv_hbm.at[0, rows], conv_ref.at[rows], sems.at[part])

    @pl.when(step == 0)
    def _():
        for part in range(conv_ref.shape[0] // BAND):
            move(part).start()
        leaf = (gathered(want_ref[...], back_ref) + held_ref[...].astype(F32)).astype(BF16)
        expanded = gelu_twice(dot(leaf, we_ref[...])).astype(BF16)
        pixels = (0.5 * dot(expanded, wp_ref[...])).astype(BF16)
        for c in range(2):
            for r in range(2):
                lanes = slice(r * LANES, (r + 1) * LANES)
                pix_ref[c, :LEAVES, lanes] = pixels[:, (2 * r + c) * LANES : (2 * r + c + 1) * LANES]
            pix_ref[c, LEAVES:, :] = jnp.zeros((GROUP, D), BF16)

    def added(index, first):
        rows = pl.ds(pl.multiple_of(first, ALIGN), GROUP)
        spots = block_ref[rows, :].T[0:1, :] - (index * TILE).astype(F32)
        spots = jnp.concatenate([spots, spots + 1.0], axis=1).astype(I32)
        hot = jnp.where(iota((TILE, 2 * GROUP), 0) == spots, 1.0, 0.0).astype(BF16)
        return dot(hot, jnp.concatenate([pix_ref[0, rows, :], pix_ref[1, rows, :]], axis=0))

    def held_rows(pair):
        row = step * BAND + 2 * pair
        return jnp.concatenate([conv_ref[row], conv_ref[row + 1]], axis=1).astype(F32)

    def store(pair, total):
        out_ref[0, 2 * pair] = total[:, :LANES].astype(BF16)
        out_ref[0, 2 * pair + 1] = total[:, LANES:].astype(BF16)

    move(step).wait()
    crowded = False
    pairs = []
    for pair in range(BAND // 2):
        index = step * (BAND // 2) + pair
        first = start_ref[0, index] // ALIGN * ALIGN
        end = start_ref[0, index + 1]
        crowded = (end > first + GROUP) | crowded
        pairs.append((pair, index, first, end))
        store(pair, held_rows(pair) + added(index, first))

    @pl.when(crowded)
    def _():
        for pair, index, first, end in pairs:
            more = lambda part, total, index=index, first=first: total + added(index, first + part * GROUP)
            store(pair, lax.fori_loop(0, (end - first + GROUP - 1) // GROUP, more, held_rows(pair)))


def call_field(starts, conv, back, held, want, block, w_expand, w_pixels):
    rows, cols, channels = conv.shape[1:]
    whole = lambda *shape: pl.BlockSpec(shape, lambda i, s: (0,) * len(shape))
    strip = pl.BlockSpec((1, BAND, cols, channels), lambda i, s: (0, i, 0, 0))
    return pl.pallas_call(
        field_kernel,
        grid_spec=pltpu.PrefetchScalarGridSpec(
            num_scalar_prefetch=1,
            grid=(rows // BAND,),
            in_specs=[
                pl.BlockSpec(memory_space=pltpu.HBM),
                whole(BACK, D),
                whole(LEAVES, D),
                whole(LEAVES, LANES),
                whole(LEAVES + GROUP, LANES),
                whole(D, D),
                whole(D, 4 * LANES),
            ],
            out_specs=strip,
            scratch_shapes=[
                pltpu.VMEM((2, LEAVES + GROUP, D), BF16),
                pltpu.VMEM(conv.shape[1:], BF16),
                pltpu.SemaphoreType.DMA((rows // BAND,)),
            ],
        ),
        out_shape=jax.ShapeDtypeStruct(conv.shape, BF16),
        compiler_params=pltpu.CompilerParams(vmem_limit_bytes=32 * 2**20),
        cost_estimate=pl.CostEstimate(flops=2 * 10**9, bytes_accessed=10 * 2**20, transcendentals=2**17),
    )(starts, kept(conv), back, held, want, block, w_expand, w_pixels)


def exchange(rows, capacity):
    width = rows.shape[1]
    blocks = rows.reshape(DEVICES, capacity, width)
    moved = lax.all_to_all(blocks, ("tile", "intra"), split_axis=0, concat_axis=0, tiled=True)
    return moved.reshape(DEVICES * capacity, width)


def shards(
    leaves,
    window_a,
    window_b,
    parent,
    coarse,
    w_query,
    w_key,
    w_value,
    w_out,
    w_up,
    w_down,
    gain_attn,
    gain_mlp,
    w_expand,
    w_pixels,
    conv_weight,
):
    weights = (w_query, w_key, w_value, w_out, w_up, w_down, gain_attn, gain_mlp)
    count = lax.axis_size("intra")
    rows = coarse.shape[1]
    head = lax.ppermute(coarse[:, rows - 1 :], "intra", [(i, i + 1) for i in range(count - 1)])
    foot = lax.ppermute(coarse[:, :1], "intra", [(i + 1, i) for i in range(count - 1)])
    sent, ret = pl.pallas_call(
        send_kernel,
        out_shape=[jax.ShapeDtypeStruct((SLOTS, WIDE), BF16), jax.ShapeDtypeStruct((8, LEAVES), I32)],
        in_specs=[pl.BlockSpec(memory_space=pltpu.HBM)] * 3,
        out_specs=[VMEM] * 2,
        scratch_shapes=[
            pltpu.VMEM((LEAVES, D), BF16),
            pltpu.VMEM((1, LEAVES), I32),
            pltpu.VMEM((1, LEAVES), I32),
            pltpu.SemaphoreType.DMA((3,)),
        ],
        compiler_params=pltpu.CompilerParams(vmem_limit_bytes=24 * 2**20),
        cost_estimate=pl.CostEstimate(flops=10**9, bytes_accessed=2**20, transcendentals=0),
    )(*map(kept, (leaves, window_a.reshape(1, LEAVES), window_b.reshape(1, LEAVES))))
    rows_a = exchange(sent, CAP)
    want, block, starts = call_order(ret, parent.reshape(1, LEAVES))
    rows_a, want, head, foot = lax.optimization_barrier((rows_a, want, head, foot))
    (sent_b,) = call_layer(
        layer_a_kernel, [jax.ShapeDtypeStruct((SLOTS, WIDE), BF16)], rows_a, weights
    )
    rows_b = exchange(sent_b, CAP)
    conv = call_conv(coarse, head, foot, conv_weight)
    rows_b, conv = lax.optimization_barrier((rows_b, conv))
    home, y, slot, rounds = call_layer(
        layer_b_kernel,
        [
            jax.ShapeDtypeStruct((BACK, D), BF16),
            jax.ShapeDtypeStruct((SLOTS, D), BF16),
            jax.ShapeDtypeStruct((8, SLOTS), I32),
            jax.ShapeDtypeStruct((1,), I32),
        ],
        rows_b,
        weights,
    )
    back = exchange(home, RET)
    total = rounds.reshape(())

    def more(state):
        return state[0] < total

    def again(state):
        turn, held = state
        index = turn.reshape(1)
        smem = pl.BlockSpec(memory_space=pltpu.SMEM)
        part = pl.pallas_call(
            resend_kernel,
            out_shape=jax.ShapeDtypeStruct((BACK, D), BF16),
            in_specs=[smem, VMEM, VMEM],
            out_specs=VMEM,
        )(index, y, slot)
        held = pl.pallas_call(
            regather_kernel,
            out_shape=jax.ShapeDtypeStruct((LEAVES, D), BF16),
            in_specs=[smem, VMEM, VMEM, VMEM],
            out_specs=VMEM,
        )(index, exchange(part, RET), want, held)
        return turn + 1, held

    _, held = lax.while_loop(more, again, (jnp.asarray(1, I32), jnp.zeros((LEAVES, D), BF16)))
    return call_field(starts, conv, back, held, want, block, w_expand, w_pixels)


def solution(mesh):
    placed = (
        P(("tile", "intra"), None),
        P(("tile", "intra")),
        P(("tile", "intra")),
        P(("tile", "intra")),
        P("tile", "intra", None, None),
    ) + (P(),) * 11
    return jax.shard_map(
        shards,
        mesh=mesh,
        in_specs=placed,
        out_specs=P("tile", "intra", None, None),
        check_vma=False,
    )
```

```python
import functools
import math

import jax
import jax.numpy as jnp
from jax import lax
from jax.experimental import pallas as pl
from jax.experimental.pallas import tpu as pltpu
from jax.sharding import PartitionSpec as P

HEADS = 4
HEAD_DIM = 64
EPSILON = 1e-06
NEGATIVE = -1e30
LOG2E = math.log2(math.e)
GELU = math.sqrt(2.0 / math.pi)
D = 256
LANES = 128
WIDE = D + LANES
DEVICES = 128
CAP = 8
SLOTS = DEVICES * CAP
LEAVES = 512
RET = 16
BACK = DEVICES * RET
FEW = 640
LIKELY = 544
GROUP = 64
ALIGN = 16
SPAN = 1024
BAND = 16
TILE = 256
FF = 1024
F32 = jnp.float32
BF16 = jnp.bfloat16
I32 = jnp.int32

VMEM = pl.BlockSpec(memory_space=pltpu.VMEM)


def kept(array):
    return pltpu.with_memory_space_constraint(array, pltpu.HBM)


def iota(shape, dim):
    return lax.broadcasted_iota(I32, shape, dim)


def fiota(shape, dim):
    return iota(shape, dim).astype(F32)


def dot(a, b):
    return jnp.dot(a, b, preferred_element_type=F32)


def dot_nt(a, b):
    return lax.dot_general(a, b, (((1,), (1,)), ((), ())), preferred_element_type=F32)


def columns(row, count):
    return jnp.broadcast_to(row, (LANES, count)).T


def onehot_rows(first, rows, targets):
    want = iota((rows, targets.shape[1]), 0) + first
    return jnp.where(want == targets, 1.0, 0.0).astype(BF16)


def send_kernel(leaves_hbm, wa_hbm, wb_hbm, out_ref, ret_ref, leaves_ref, wa_ref, wb_ref, sems):
    moves = [
        pltpu.make_async_copy(source, target, sems.at[index])
        for index, (source, target) in enumerate(((wa_hbm, wa_ref), (wb_hbm, wb_ref), (leaves_hbm, leaves_ref)))
    ]
    for move in moves:
        move.start()
    moves[0].wait()
    moves[1].wait()
    a_row = wa_ref[...].astype(F32)
    b_row = wb_ref[...].astype(F32)
    a_col = columns(a_row, LEAVES)
    b_col = columns(b_row, LEAVES)
    l_col = fiota((LEAVES, LANES), 0)
    key_col = a_col * LEAVES + l_col
    slots = []
    ranks = []
    for part in range(LEAVES // LANES):
        lanes = slice(part * LANES, (part + 1) * LANES)
        ar = a_row[:, lanes]
        br = b_row[:, lanes]
        lr = fiota((1, LANES), 1) + part * LANES
        same_a = jnp.where(a_col == ar, jnp.where(l_col < lr, 1.0, 0.0), 0.0)
        same_b = jnp.where(b_col == br, jnp.where(key_col < ar * LEAVES + lr, 1.0, 0.0), 0.0)
        slots.append(ar * CAP + jnp.sum(same_a, axis=0, keepdims=True))
        ranks.append(jnp.sum(same_b, axis=0, keepdims=True))
    slot = jnp.concatenate(slots, axis=1).astype(I32)
    rank = jnp.concatenate(ranks, axis=1)
    turn = jnp.floor(rank * (1.0 / RET))
    ret = b_row * RET + (rank - turn * RET) + turn * BACK
    ret_ref[...] = jnp.broadcast_to(ret, (8, LEAVES)).astype(I32)
    rounds = jnp.max(turn) + 1.0
    lane = iota((LEAVES, LANES), 1)
    turn_col = columns(slot.astype(F32), LEAVES) - a_col * CAP
    held = jnp.where(turn_col == lane.astype(F32), b_col + 1.0, 0.0).astype(BF16)
    tags = dot(onehot_rows(0, DEVICES, a_row.astype(I32)), held)
    tags = jnp.where(iota((DEVICES, LANES), 1) == CAP, rounds, tags).astype(BF16)
    in_a = jnp.where(a_col == lane.astype(F32), 1.0, 0.0).astype(BF16)
    counts = dot(onehot_rows(0, DEVICES, b_row.astype(I32)), in_a).astype(BF16)
    line = iota((SLOTS, LANES), 0)
    spread = jnp.where(line // CAP == iota((SLOTS, LANES), 1), 1.0, 0.0).astype(BF16)
    extra = jnp.where(line % CAP == 0, dot(spread, tags), jnp.where(line % CAP == 1, dot(spread, counts), 0.0))
    out_ref[:, D:] = extra.astype(BF16)
    moves[2].wait()
    for first in range(0, SLOTS, SPAN):
        hot = onehot_rows(first, SPAN, slot)
        out_ref[first : first + SPAN, :D] = dot(hot, leaves_ref[...]).astype(BF16)


def message_rows(x_ref, which):
    pick = iota((DEVICES, SLOTS), 0) * CAP + which == iota((DEVICES, SLOTS), 1)
    return dot(jnp.where(pick, 1.0, 0.0).astype(BF16), x_ref[:, D:])


def interleave(by_turn):
    spread = jnp.where(iota((DEVICES, SLOTS), 1) // CAP == iota((DEVICES, SLOTS), 0), 1.0, 0.0).astype(BF16)
    wide = dot(by_turn.astype(BF16), spread)
    own = iota((CAP, SLOTS), 1) % CAP == iota((CAP, SLOTS), 0)
    return jnp.sum(jnp.where(own, wide, 0.0), axis=0, keepdims=True)


def ranks_of(tag_row, tag_col):
    ranks = []
    for part in range(tag_row.shape[1] // LANES):
        row = tag_row[:, part * LANES : (part + 1) * LANES]
        block = tag_col[part * LANES : (part + 1) * LANES, :]
        before = iota((LANES, LANES), 0) < iota((LANES, LANES), 1)
        hits = jnp.where(before, jnp.where(block == row, 1.0, 0.0), 0.0)
        rank = jnp.sum(hits, axis=0, keepdims=True)
        if part:
            above = jnp.where(tag_col[: part * LANES, :] == row, 1.0, 0.0)
            rank = rank + jnp.sum(above, axis=0, keepdims=True)
        ranks.append(rank)
    return jnp.concatenate(ranks, axis=1)


def rms(values, gain):
    mean_sq = jnp.mean(values * values, axis=-1, keepdims=True)
    return (values * lax.rsqrt(mean_sq + EPSILON) * gain).astype(BF16)


def fetch(layer_index, sources, targets, sems):
    moves = []
    for index, (source, target) in enumerate(zip(sources, targets)):
        part = source if index >= 6 else source.at[layer_index]
        moves.append(pltpu.make_async_copy(part, target, sems.at[index]))
        moves[-1].start()
    return moves


def gelu_twice(x):
    inner = x * (x * x * (0.044715 * GELU) + GELU)
    return x + x * jnp.tanh(inner)


def layer(layer_index, count, tile, asked, x_ref, live, weights, y_ref, q_ref, k_ref, v_ref, live_ref):
    wq, wk, wv, wo, wu, wd, gain_one, gain_two = weights
    one = gain_one[layer_index : layer_index + 1, :]
    two = gain_two[layer_index : layer_index + 1, :]
    low = iota((tile, LANES), 1) < HEAD_DIM
    zero = jnp.asarray(0, BF16)
    live_ref[:count, :] = live.astype(BF16)
    first = dot(rms(x_ref[:ALIGN, :D].astype(F32), one), wk[...])[0:1, :].astype(BF16)

    def project(step, _):
        rows = pl.ds(pl.multiple_of(step * tile, tile), tile)
        normed = rms(x_ref[rows, :D].astype(F32), one)
        flag = live_ref[rows, :]
        q_ref[rows, :] = (dot(normed, wq[...]) * (HEAD_DIM**-0.5 * LOG2E)).astype(BF16)
        key = dot(normed, wk[...]).astype(BF16)
        k_ref[rows, :] = jnp.where(jnp.concatenate([flag, flag], axis=1) > 0, key, first)
        value = dot(normed, wv[...]).astype(BF16)
        for pair in range(HEADS // 2):
            part = value[:, pair * LANES : (pair + 1) * LANES]
            lanes = slice(pair * LANES, (pair + 1) * LANES)
            v_ref[2 * pair, rows, lanes] = jnp.where(low, part, flag)
            v_ref[2 * pair + 1, rows, lanes] = jnp.where(low, flag, part)
            other = slice((1 - pair) * LANES, (2 - pair) * LANES)
            v_ref[2 * pair, rows, other] = flag
            v_ref[2 * pair + 1, rows, other] = flag
        return 0

    lax.fori_loop(0, count // tile, project, 0)

    tile = asked[1]
    low = iota((tile, LANES), 1) < HEAD_DIM

    def attend(step, _):
        rows = pl.ds(pl.multiple_of(step * tile, ALIGN), tile)

        def scored(head):
            lanes = slice(head // 2 * LANES, (head // 2 + 1) * LANES)
            query = q_ref[rows, lanes]
            own = jnp.where(low, query, zero) if head % 2 == 0 else jnp.where(low, zero, query)
            return dot_nt(own, k_ref[:count, lanes])

        def mixed(head, scores):
            peak = jnp.max(scores, axis=-1, keepdims=True)
            lanes = slice(head // 2 * LANES, (head // 2 + 1) * LANES)
            return dot(jnp.exp2(scores - peak).astype(BF16), v_ref[head, :count, :])[:, lanes]

        ahead = scored(0)
        outs = []
        for head in range(HEADS):
            scores = ahead
            if head + 1 < HEADS:
                ahead = scored(head + 1)
            outs.append(mixed(head, scores))
        parts = []
        for pair in range(HEADS // 2):
            even, odd = outs[2 * pair : 2 * pair + 2]
            total = pltpu.roll(jnp.where(low, odd, even), HEAD_DIM, 1)
            parts.append(jnp.where(low, even, odd) / total)
        att = jnp.concatenate(parts, axis=1).astype(BF16)
        hidden = x_ref[rows, :D].astype(F32) + dot(att, wo[...])
        up = gelu_twice(dot(rms(hidden, two), wu[...])).astype(BF16)
        y_ref[rows, :] = (hidden + 0.5 * dot(up, wd[...])).astype(BF16)
        return 0

    lax.fori_loop(0, asked[0] // tile, attend, 0)


def layer_a_kernel(x_ref, *refs):
    sources, out_ref, weights, sems, (y_ref, *rest) = refs[:8], refs[8], refs[9:17], refs[17], refs[18:]
    moves = fetch(0, sources, weights, sems)
    tags = message_rows(x_ref, 0)
    picks = jnp.where(iota((CAP, LANES), 0) == iota((CAP, LANES), 1), 1.0, 0.0).astype(BF16)
    tag_row = interleave(dot_nt(picks, tags.astype(BF16)))
    tag_col = columns(tag_row, SLOTS)
    slot = (tag_row - 1.0) * CAP + ranks_of(tag_row, tag_col)
    slot = jnp.where(tag_row > 0.0, slot, -1.0).astype(I32)
    for move in moves:
        move.wait()
    live = jnp.where(tag_col > 0.0, 1.0, 0.0)
    layer(0, SLOTS, 2 * TILE, (SLOTS, 2 * TILE), x_ref, live, weights, y_ref, *rest)
    out_ref[...] = dot(onehot_rows(0, SLOTS, slot), y_ref[...]).astype(BF16)


def before(flags):
    parts = flags.shape[1] // LANES
    square = jnp.concatenate([flags[:, p * LANES : (p + 1) * LANES] for p in range(parts)], axis=0)
    upper = jnp.where(iota((LANES, LANES), 0) < iota((LANES, LANES), 1), 1.0, 0.0).astype(BF16)
    inner = dot(square.astype(BF16), upper)
    held = jnp.zeros((1, 1), F32)
    rows = []
    for p in range(parts):
        rows.append(inner[p : p + 1, :] + held)
        held = held + jnp.sum(square[p : p + 1, :], axis=1, keepdims=True)
    return jnp.concatenate(rows, axis=1)


def plan_kernel(x_ref, place_ref, slot_ref, live_ref, total_ref, rounds_ref):
    tags = message_rows(x_ref, 0)
    rounds_ref[0] = jnp.max(jnp.where(iota((DEVICES, LANES), 1) == CAP, tags, 0.0)).astype(I32)
    counts = message_rows(x_ref, 1)
    lower = jnp.where(iota((DEVICES, DEVICES), 0) >= iota((DEVICES, DEVICES), 1), 1.0, 0.0).astype(BF16)
    running = dot(lower, counts.astype(BF16))
    homes = []
    for turn in range(CAP):
        home = jnp.sum(jnp.where(running <= turn, 1.0, 0.0), axis=0, keepdims=True)
        homes.append(jnp.where(home < DEVICES, home + 1.0, 0.0))
    tag = interleave(jnp.concatenate(homes, axis=0))
    live = jnp.where(tag > 0.0, 1.0, 0.0)
    total_ref[0] = jnp.sum(live).astype(I32)
    place = jnp.where(tag > 0.0, before(live), -1.0).astype(I32)
    place_ref[...] = jnp.broadcast_to(place, (8, SLOTS))
    tag_col = dot(onehot_rows(0, SLOTS, place), columns(tag, SLOTS).astype(BF16))
    tag_row = tag_col.T[0:1, :]
    rank = ranks_of(tag_row, tag_col)
    turn = jnp.floor(rank * (1.0 / RET))
    slot = (tag_row - 1.0) * RET + (rank - turn * RET) + turn * BACK
    slot = jnp.where(tag_row > 0.0, slot, -1.0).astype(I32)
    slot_ref[...] = jnp.broadcast_to(slot, (8, SLOTS))
    flag = jnp.where(iota((SLOTS, LANES), 0) == 0, 1.0, jnp.where(tag_col > 0.0, 1.0, 0.0))
    live_ref[...] = flag.astype(BF16)


def call_plan(rows):
    smem = pl.BlockSpec(memory_space=pltpu.SMEM)
    return pl.pallas_call(
        plan_kernel,
        out_shape=[
            jax.ShapeDtypeStruct((8, SLOTS), I32),
            jax.ShapeDtypeStruct((8, SLOTS), I32),
            jax.ShapeDtypeStruct((SLOTS, LANES), BF16),
            jax.ShapeDtypeStruct((1,), I32),
            jax.ShapeDtypeStruct((1,), I32),
        ],
        in_specs=[VMEM],
        out_specs=[VMEM, VMEM, VMEM, smem, smem],
        compiler_params=pltpu.CompilerParams(vmem_limit_bytes=24 * 2**20),
        cost_estimate=pl.CostEstimate(flops=2 * 10**9, bytes_accessed=2**20, transcendentals=0),
    )(rows)


def finish_b(count, tile, asked, x_ref, place_ref, slot_ref, flag_ref, packed_ref, weights, moves, refs):
    out_ref, y_ref, *rest = refs
    packed_ref[:count, :] = dot(onehot_rows(0, count, place_ref[0:1, :]), x_ref[...]).astype(BF16)
    if count < SLOTS:
        y_ref[asked[0] :, :] = jnp.zeros((SLOTS - asked[0], D), BF16)
    for move in moves:
        move.wait()
    layer(1, count, tile, asked, packed_ref, flag_ref[:count, :], weights, y_ref, *rest)
    for first in range(0, BACK, SPAN):
        hot = onehot_rows(first, SPAN, slot_ref[0:1, :count])
        out_ref[first : first + SPAN, :] = dot(hot, y_ref[:count, :]).astype(BF16)


def layer_b_kernel(x_ref, place_ref, slot_ref, flag_ref, total_ref, *refs):
    sources, (out_ref, y_ref, held_ref) = refs[:8], refs[8:11]
    weights, sems, (packed_ref, *rest) = refs[11:19], refs[19], refs[20:]
    moves = fetch(1, sources, weights, sems)
    held_ref[...] = jnp.zeros(held_ref.shape, BF16)
    given = (x_ref, place_ref, slot_ref, flag_ref, packed_ref, weights, moves, (out_ref, y_ref, *rest))

    @pl.when(total_ref[0] <= LIKELY)
    def _():
        finish_b(FEW, FEW // 2, (LIKELY, LIKELY // 2), *given)

    @pl.when(total_ref[0] > LIKELY)
    def _():
        finish_b(SLOTS, TILE, (SLOTS, TILE), *given)


def call_layer(kernel, out_shape, rows, plan, weights):
    kernel_weights = [pltpu.VMEM(weight.shape[1:], BF16) for weight in weights[:6]]
    kernel_weights += [pltpu.VMEM(gain.shape, F32) for gain in weights[6:]]
    scratch = [
        pltpu.VMEM((SLOTS, D), BF16),
        pltpu.VMEM((SLOTS, D), BF16),
        pltpu.VMEM((SLOTS, D), BF16),
        pltpu.VMEM((HEADS, SLOTS, D), BF16),
        pltpu.VMEM((SLOTS, LANES), BF16),
    ]
    smem = pl.BlockSpec(memory_space=pltpu.SMEM)
    return pl.pallas_call(
        kernel,
        out_shape=out_shape,
        in_specs=[VMEM] + [smem if part.shape == (1,) else VMEM for part in plan]
        + [pl.BlockSpec(memory_space=pltpu.HBM)] * 8,
        out_specs=[VMEM] * len(out_shape),
        scratch_shapes=kernel_weights + [pltpu.SemaphoreType.DMA((8,))] + scratch,
        compiler_params=pltpu.CompilerParams(vmem_limit_bytes=24 * 2**20),
        cost_estimate=pl.CostEstimate(flops=6 * 10**9, bytes_accessed=4 * 2**20, transcendentals=5 * 2**20),
    )(rows, *plan, *map(kept, weights))


def resend_kernel(turn_ref, y_ref, slot_ref, out_ref):
    slot = slot_ref[0:1, :] - turn_ref[0] * BACK
    for first in range(0, BACK, TILE):
        hot = onehot_rows(first, TILE, slot)
        out_ref[first : first + TILE, :] = dot(hot, y_ref[...]).astype(BF16)


def gathered(want, back_ref):
    parts = []
    for first in range(0, LEAVES, LANES):
        block = want[first : first + LANES, :]
        hot = jnp.concatenate(
            [
                jnp.where(block == iota((LANES, LANES), 1) + lanes, 1.0, 0.0).astype(BF16)
                for lanes in range(0, BACK, LANES)
            ],
            axis=1,
        )
        parts.append(dot(hot, back_ref[...]))
    return jnp.concatenate(parts, axis=0)


def regather_kernel(turn_ref, back_ref, want_ref, held_ref, out_ref):
    rows = gathered(want_ref[...] - turn_ref[0] * BACK, back_ref)
    out_ref[...] = (held_ref[...].astype(F32) + rows).astype(BF16)


def order_kernel(ret_ref, parent_ref, want_ref, again_ref, block_ref, start_ref):
    parent = parent_ref[...].astype(F32)
    ret = ret_ref[0:1, :].astype(F32)
    p_col = columns(parent, LEAVES)
    l_col = fiota((LEAVES, LANES), 0)
    parts = []
    for part in range(LEAVES // LANES):
        pr = parent[:, part * LANES : (part + 1) * LANES]
        lr = fiota((1, LANES), 1) + part * LANES
        less = jnp.where(p_col * LEAVES + l_col < pr * LEAVES + lr, 1.0, 0.0)
        parts.append(jnp.sum(less, axis=0, keepdims=True))
    place = jnp.concatenate(parts, axis=1)
    for first in range(0, LEAVES, LANES):
        rows = slice(first, first + LANES)
        hit = place == fiota((LANES, LEAVES), 0) + first
        want = jnp.sum(jnp.where(hit, ret, 0.0), axis=1, keepdims=True)
        want_ref[rows, :] = jnp.broadcast_to(want, (LANES, LANES)).astype(I32)
        again_ref[rows, :] = want_ref[rows, :]
        block = 2.0 * jnp.sum(jnp.where(hit, parent, 0.0), axis=1, keepdims=True)
        block_ref[rows, :] = jnp.broadcast_to(block, (LANES, LANES))
    block_ref[LEAVES:, :] = jnp.full((GROUP, LANES), -8.0, F32)
    below = jnp.where(p_col < fiota((1, LANES), 1) * LANES, 1.0, 0.0)
    start_ref[...] = jnp.broadcast_to(jnp.sum(below, axis=0, keepdims=True), (8, LANES)).astype(I32)


def call_order(ret, parent):
    return pl.pallas_call(
        order_kernel,
        out_shape=[
            jax.ShapeDtypeStruct((LEAVES, LANES), I32),
            jax.ShapeDtypeStruct((LEAVES, LANES), I32),
            jax.ShapeDtypeStruct((LEAVES + GROUP, LANES), F32),
            jax.ShapeDtypeStruct((8, LANES), I32),
        ],
        in_specs=[VMEM, VMEM],
        out_specs=[VMEM] * 4,
        compiler_params=pltpu.CompilerParams(vmem_limit_bytes=24 * 2**20),
        cost_estimate=pl.CostEstimate(flops=10**9, bytes_accessed=2**20, transcendentals=0),
    )(ret, parent)


STRIP = 8


def conv_kernel(count, main_ref, above_ref, below_ref, head_ref, foot_ref, weight_ref, out_ref, w_ref):
    step = pl.program_id(0)

    @pl.when(step == 0)
    def _():
        zero = jnp.zeros((LANES, LANES), BF16)
        for b in range(3):
            for row in range(4):
                for r in range(2):
                    block = weight_ref[row - r, b] if 0 <= row - r < 3 else zero
                    w_ref[b, row * LANES : (row + 1) * LANES, r * LANES : (r + 1) * LANES] = block

    above = jnp.where(step == 0, head_ref[0, 0], above_ref[0, 0])
    below = jnp.where(step == count - 1, foot_ref[0, 0], below_ref[0, 0])
    rows = [above] + [main_ref[0, r] for r in range(STRIP)] + [below]
    column = iota((TILE, TILE), 0)
    for pair in range(STRIP // 2):
        wide = jnp.concatenate(rows[2 * pair : 2 * pair + 4], axis=1)
        left = pltpu.roll(dot(wide, w_ref[0]), 1, 0)
        right = pltpu.roll(dot(wide, w_ref[2]), TILE - 1, 0)
        both = dot(wide, w_ref[1])
        both = both + jnp.where(column == 0, 0.0, left) + jnp.where(column == TILE - 1, 0.0, right)
        out_ref[0, 2 * pair] = both[:, :LANES].astype(BF16)
        out_ref[0, 2 * pair + 1] = both[:, LANES:].astype(BF16)


def call_conv(coarse, head, foot, weight):
    rows, cols, channels = coarse.shape[1:]
    count = rows // STRIP
    single = (1, 1, cols, channels)
    return pl.pallas_call(
        functools.partial(conv_kernel, count),
        grid=(count,),
        out_shape=jax.ShapeDtypeStruct(coarse.shape, BF16),
        in_specs=[
            pl.BlockSpec((1, STRIP, cols, channels), lambda i: (0, i, 0, 0)),
            pl.BlockSpec(single, lambda i: (0, jnp.maximum(i * STRIP - 1, 0), 0, 0)),
            pl.BlockSpec(single, lambda i: (0, jnp.minimum(i * STRIP + STRIP, rows - 1), 0, 0)),
            pl.BlockSpec(single, lambda i: (0, 0, 0, 0)),
            pl.BlockSpec(single, lambda i: (0, 0, 0, 0)),
            pl.BlockSpec(weight.shape, lambda i: (0, 0, 0, 0)),
        ],
        out_specs=pl.BlockSpec((1, STRIP, cols, channels), lambda i: (0, i, 0, 0)),
        scratch_shapes=[pltpu.VMEM((3, 4 * LANES, 2 * LANES), BF16)],
        compiler_params=pltpu.CompilerParams(vmem_limit_bytes=24 * 2**20),
        cost_estimate=pl.CostEstimate(flops=6 * 10**9, bytes_accessed=8 * 2**20, transcendentals=0),
    )(*[kept(coarse)] * 3, head, foot, weight)


def field_kernel(start_ref, conv_hbm, held_hbm, rounds_ref, back_ref, want_ref, block_ref, we_ref, wp_ref, out_ref, pix_ref, conv_ref, held_ref, sems, held_sem):
    step = pl.program_id(0)

    def move(part):
        rows = pl.ds(part * BAND, BAND)
        return pltpu.make_async_copy(conv_hbm.at[0, rows], conv_ref.at[rows], sems.at[part])

    @pl.when(step == 0)
    def _():
        for part in range(conv_ref.shape[0] // BAND):
            move(part).start()
        held_ref[...] = jnp.zeros(held_ref.shape, BF16)

        @pl.when(rounds_ref[0] > 1)
        def _():
            load = pltpu.make_async_copy(held_hbm, held_ref, held_sem.at[0])
            load.start()
            load.wait()

        leaf = (gathered(want_ref[...], back_ref) + held_ref[...].astype(F32)).astype(BF16)
        expanded = gelu_twice(dot(leaf, we_ref[...])).astype(BF16)
        pixels = (0.5 * dot(expanded, wp_ref[...])).astype(BF16)
        for c in range(2):
            for r in range(2):
                lanes = slice(r * LANES, (r + 1) * LANES)
                pix_ref[c, :LEAVES, lanes] = pixels[:, (2 * r + c) * LANES : (2 * r + c + 1) * LANES]
            pix_ref[c, LEAVES:, :] = jnp.zeros((GROUP, D), BF16)

    def added(index, first):
        rows = pl.ds(pl.multiple_of(first, ALIGN), GROUP)
        spots = block_ref[rows, :].T[0:1, :] - (index * TILE).astype(F32)
        spots = jnp.concatenate([spots, spots + 1.0], axis=1).astype(I32)
        hot = jnp.where(iota((TILE, 2 * GROUP), 0) == spots, 1.0, 0.0).astype(BF16)
        return dot(hot, jnp.concatenate([pix_ref[0, rows, :], pix_ref[1, rows, :]], axis=0))

    def held_rows(pair):
        row = step * BAND + 2 * pair
        return jnp.concatenate([conv_ref[row], conv_ref[row + 1]], axis=1).astype(F32)

    def store(pair, total):
        out_ref[0, 2 * pair] = total[:, :LANES].astype(BF16)
        out_ref[0, 2 * pair + 1] = total[:, LANES:].astype(BF16)

    move(step).wait()
    crowded = False
    pairs = []
    for pair in range(BAND // 2):
        index = step * (BAND // 2) + pair
        first = start_ref[0, index] // ALIGN * ALIGN
        end = start_ref[0, index + 1]
        crowded = (end > first + GROUP) | crowded
        pairs.append((pair, index, first, end))
        store(pair, held_rows(pair) + added(index, first))

    @pl.when(crowded)
    def _():
        for pair, index, first, end in pairs:
            more = lambda part, total, index=index, first=first: total + added(index, first + part * GROUP)
            store(pair, lax.fori_loop(0, (end - first + GROUP - 1) // GROUP, more, held_rows(pair)))


def call_field(starts, conv, held, rounds, back, want, block, w_expand, w_pixels):
    rows, cols, channels = conv.shape[1:]
    strip = pl.BlockSpec((1, BAND, cols, channels), lambda i, s: (0, i, 0, 0))
    return pl.pallas_call(
        field_kernel,
        grid_spec=pltpu.PrefetchScalarGridSpec(
            num_scalar_prefetch=1,
            grid=(rows // BAND,),
            in_specs=[
                pl.BlockSpec(memory_space=pltpu.HBM),
                pl.BlockSpec(memory_space=pltpu.HBM),
                pl.BlockSpec(memory_space=pltpu.SMEM),
            ]
            + [VMEM] * 5,
            out_specs=strip,
            scratch_shapes=[
                pltpu.VMEM((2, LEAVES + GROUP, D), BF16),
                pltpu.VMEM(conv.shape[1:], BF16),
                pltpu.VMEM((LEAVES, D), BF16),
                pltpu.SemaphoreType.DMA((rows // BAND,)),
                pltpu.SemaphoreType.DMA((1,)),
            ],
        ),
        out_shape=jax.ShapeDtypeStruct(conv.shape, BF16),
        compiler_params=pltpu.CompilerParams(vmem_limit_bytes=32 * 2**20),
        cost_estimate=pl.CostEstimate(flops=2 * 10**9, bytes_accessed=10 * 2**20, transcendentals=2**17),
    )(starts, kept(conv), kept(held), rounds, back, want, block, w_expand, w_pixels)


def exchange(rows, capacity):
    width = rows.shape[1]
    blocks = rows.reshape(DEVICES, capacity, width)
    moved = lax.all_to_all(blocks, ("tile", "intra"), split_axis=0, concat_axis=0, tiled=True)
    return moved.reshape(DEVICES * capacity, width)


def shards(
    leaves,
    window_a,
    window_b,
    parent,
    coarse,
    w_query,
    w_key,
    w_value,
    w_out,
    w_up,
    w_down,
    gain_attn,
    gain_mlp,
    w_expand,
    w_pixels,
    conv_weight,
):
    weights = (w_query, w_key, w_value, w_out, w_up, w_down, gain_attn, gain_mlp)
    count = lax.axis_size("intra")
    rows = coarse.shape[1]
    head = lax.ppermute(coarse[:, rows - 1 :], "intra", [(i, i + 1) for i in range(count - 1)])
    foot = lax.ppermute(coarse[:, :1], "intra", [(i + 1, i) for i in range(count - 1)])
    sent, ret = pl.pallas_call(
        send_kernel,
        out_shape=[jax.ShapeDtypeStruct((SLOTS, WIDE), BF16), jax.ShapeDtypeStruct((8, LEAVES), I32)],
        in_specs=[pl.BlockSpec(memory_space=pltpu.HBM)] * 3,
        out_specs=[VMEM] * 2,
        scratch_shapes=[
            pltpu.VMEM((LEAVES, D), BF16),
            pltpu.VMEM((1, LEAVES), I32),
            pltpu.VMEM((1, LEAVES), I32),
            pltpu.SemaphoreType.DMA((3,)),
        ],
        compiler_params=pltpu.CompilerParams(vmem_limit_bytes=24 * 2**20),
        cost_estimate=pl.CostEstimate(flops=10**9, bytes_accessed=2**20, transcendentals=0),
    )(*map(kept, (leaves, window_a.reshape(1, LEAVES), window_b.reshape(1, LEAVES))))
    rows_a = exchange(sent, CAP)
    want, again_want, block, starts = call_order(ret, parent.reshape(1, LEAVES))
    rows_a, want, head, foot = lax.optimization_barrier((rows_a, want, head, foot))
    (sent_b,) = call_layer(layer_a_kernel, [jax.ShapeDtypeStruct((SLOTS, D), BF16)], rows_a, (), weights)
    rows_b = exchange(sent_b, CAP)
    place, slot, flag, live, rounds = call_plan(rows_a)
    home, y, held = call_layer(
        layer_b_kernel,
        [
            jax.ShapeDtypeStruct((BACK, D), BF16),
            jax.ShapeDtypeStruct((SLOTS, D), BF16),
            jax.ShapeDtypeStruct((LEAVES, D), BF16),
        ],
        rows_b,
        (place, slot, flag, live),
        weights,
    )
    back = exchange(home, RET)
    total = rounds.reshape(())

    def more(state):
        return state[0] < total

    def again(state):
        turn, held = state
        index = turn.reshape(1)
        smem = pl.BlockSpec(memory_space=pltpu.SMEM)
        part = pl.pallas_call(
            resend_kernel,
            out_shape=jax.ShapeDtypeStruct((BACK, D), BF16),
            in_specs=[smem, VMEM, VMEM],
            out_specs=VMEM,
        )(index, y, slot)
        held = pl.pallas_call(
            regather_kernel,
            out_shape=jax.ShapeDtypeStruct((LEAVES, D), BF16),
            in_specs=[smem, VMEM, VMEM, VMEM],
            out_specs=VMEM,
        )(index, exchange(part, RET), again_want, held)
        return turn + 1, held

    _, held = lax.while_loop(more, again, (jnp.asarray(1, I32), held))
    head, held = lax.optimization_barrier((head, held))
    conv = call_conv(coarse, head, foot, conv_weight)
    return call_field(starts, conv, held, rounds, back, want, block, w_expand, w_pixels)


def solution(mesh):
    placed = (
        P(("tile", "intra"), None),
        P(("tile", "intra")),
        P(("tile", "intra")),
        P(("tile", "intra")),
        P("tile", "intra", None, None),
    ) + (P(),) * 11
    return jax.shard_map(
        shards,
        mesh=mesh,
        in_specs=placed,
        out_specs=P("tile", "intra", None, None),
        check_vma=False,
    )
```

```python
import functools
import math

import jax
import jax.numpy as jnp
from jax import lax
from jax.experimental import pallas as pl
from jax.experimental.pallas import tpu as pltpu
from jax.sharding import PartitionSpec as P

HEADS = 4
HEAD_DIM = 64
EPSILON = 1e-06
NEGATIVE = -1e30
LOG2E = math.log2(math.e)
GELU = math.sqrt(2.0 / math.pi)
D = 256
LANES = 128
WIDE = D + LANES
DEVICES = 128
CAP = 8
SLOTS = DEVICES * CAP
LEAVES = 512
RET = 16
BACK = DEVICES * RET
FEW = 640
LIKELY = 544
GROUP = 64
ALIGN = 16
CHUNK = 512
BAND = 16
TILE = 256
FF = 1024
F32 = jnp.float32
BF16 = jnp.bfloat16
I32 = jnp.int32

VMEM = pl.BlockSpec(memory_space=pltpu.VMEM)


def kept(array):
    return pltpu.with_memory_space_constraint(array, pltpu.HBM)


def iota(shape, dim):
    return lax.broadcasted_iota(I32, shape, dim)


def fiota(shape, dim):
    return iota(shape, dim).astype(F32)


def dot(a, b):
    return jnp.dot(a, b, preferred_element_type=F32)


def dot_nt(a, b):
    return lax.dot_general(a, b, (((1,), (1,)), ((), ())), preferred_element_type=F32)


def columns(row, count):
    return jnp.broadcast_to(row, (LANES, count)).T


def onehot_rows(first, rows, targets):
    want = iota((rows, targets.shape[1]), 0) + first
    return jnp.where(want == targets, 1.0, 0.0).astype(BF16)


def send_kernel(leaves_hbm, wa_hbm, wb_hbm, out_hbm, ret_ref, out_ref, leaves_ref, wa_ref, wb_ref, sems, left):
    moves = [
        pltpu.make_async_copy(source, target, sems.at[index])
        for index, (source, target) in enumerate(((wa_hbm, wa_ref), (wb_hbm, wb_ref), (leaves_hbm, leaves_ref)))
    ]
    for move in moves:
        move.start()
    moves[0].wait()
    moves[1].wait()
    a_row = wa_ref[...].astype(F32)
    b_row = wb_ref[...].astype(F32)
    a_col = columns(a_row, LEAVES)
    b_col = columns(b_row, LEAVES)
    l_col = fiota((LEAVES, LANES), 0)
    key_col = a_col * LEAVES + l_col
    slots = []
    ranks = []
    for part in range(LEAVES // LANES):
        lanes = slice(part * LANES, (part + 1) * LANES)
        ar = a_row[:, lanes]
        br = b_row[:, lanes]
        lr = fiota((1, LANES), 1) + part * LANES
        same_a = jnp.where(a_col == ar, jnp.where(l_col < lr, 1.0, 0.0), 0.0)
        same_b = jnp.where(b_col == br, jnp.where(key_col < ar * LEAVES + lr, 1.0, 0.0), 0.0)
        slots.append(ar * CAP + jnp.sum(same_a, axis=0, keepdims=True))
        ranks.append(jnp.sum(same_b, axis=0, keepdims=True))
    slot = jnp.concatenate(slots, axis=1).astype(I32)
    rank = jnp.concatenate(ranks, axis=1)
    turn = jnp.floor(rank * (1.0 / RET))
    ret = b_row * RET + (rank - turn * RET) + turn * BACK
    ret_ref[...] = jnp.broadcast_to(ret, (8, LEAVES)).astype(I32)
    rounds = jnp.max(turn) + 1.0
    lane = iota((LEAVES, LANES), 1)
    turn_col = columns(slot.astype(F32), LEAVES) - a_col * CAP
    held = jnp.where(turn_col == lane.astype(F32), b_col + 1.0, 0.0).astype(BF16)
    tags = dot(onehot_rows(0, DEVICES, a_row.astype(I32)), held)
    tags = jnp.where(iota((DEVICES, LANES), 1) == CAP, rounds, tags).astype(BF16)
    in_a = jnp.where(a_col == lane.astype(F32), 1.0, 0.0).astype(BF16)
    counts = dot(onehot_rows(0, DEVICES, b_row.astype(I32)), in_a).astype(BF16)
    line = iota((SLOTS, LANES), 0)
    spread = jnp.where(line // CAP == iota((SLOTS, LANES), 1), 1.0, 0.0).astype(BF16)
    extra = jnp.where(line % CAP == 0, dot(spread, tags), jnp.where(line % CAP == 1, dot(spread, counts), 0.0))
    out_ref[:, D:] = extra.astype(BF16)
    moves[2].wait()
    scatter_out(slot, leaves_ref[...], out_ref, out_hbm, left)


def message_rows(x_ref, which):
    pick = iota((DEVICES, SLOTS), 0) * CAP + which == iota((DEVICES, SLOTS), 1)
    return dot(jnp.where(pick, 1.0, 0.0).astype(BF16), x_ref[:, D:])


def interleave(by_turn):
    spread = jnp.where(iota((DEVICES, SLOTS), 1) // CAP == iota((DEVICES, SLOTS), 0), 1.0, 0.0).astype(BF16)
    wide = dot(by_turn.astype(BF16), spread)
    own = iota((CAP, SLOTS), 1) % CAP == iota((CAP, SLOTS), 0)
    return jnp.sum(jnp.where(own, wide, 0.0), axis=0, keepdims=True)


def ranks_of(tag_row, tag_col):
    ranks = []
    for part in range(tag_row.shape[1] // LANES):
        row = tag_row[:, part * LANES : (part + 1) * LANES]
        block = tag_col[part * LANES : (part + 1) * LANES, :]
        before = iota((LANES, LANES), 0) < iota((LANES, LANES), 1)
        hits = jnp.where(before, jnp.where(block == row, 1.0, 0.0), 0.0)
        rank = jnp.sum(hits, axis=0, keepdims=True)
        if part:
            above = jnp.where(tag_col[: part * LANES, :] == row, 1.0, 0.0)
            rank = rank + jnp.sum(above, axis=0, keepdims=True)
        ranks.append(rank)
    return jnp.concatenate(ranks, axis=1)


def rms(values, gain):
    mean_sq = jnp.mean(values * values, axis=-1, keepdims=True)
    return (values * lax.rsqrt(mean_sq + EPSILON) * gain).astype(BF16)


def scatter_out(slot, rows, held_ref, out_hbm, sems):
    moves = []
    for part in range(held_ref.shape[0] // CHUNK):
        lines = pl.ds(part * CHUNK, CHUNK)
        held_ref[lines, :D] = dot(onehot_rows(part * CHUNK, CHUNK, slot), rows).astype(BF16)
        moves.append(pltpu.make_async_copy(held_ref.at[lines], out_hbm.at[lines], sems.at[part]))
        moves[-1].start()
    for move in moves:
        move.wait()


def fetch(layer_index, sources, targets, sems):
    moves = []
    for index, (source, target) in enumerate(zip(sources, targets)):
        part = source if index >= 6 else source.at[layer_index]
        moves.append(pltpu.make_async_copy(part, target, sems.at[index]))
        moves[-1].start()
    return moves


def gelu_twice(x):
    inner = x * (x * x * (0.044715 * GELU) + GELU)
    return x + x * jnp.tanh(inner)


def layer(layer_index, count, tile, asked, unroll, x_ref, live, weights, y_ref, q_ref, k_ref, v_ref, live_ref):
    wq, wk, wv, wo, wu, wd, gain_one, gain_two = weights
    one = gain_one[layer_index : layer_index + 1, :]
    two = gain_two[layer_index : layer_index + 1, :]
    low = iota((tile, LANES), 1) < HEAD_DIM
    zero = jnp.asarray(0, BF16)
    live_ref[:count, :] = live.astype(BF16)
    first = dot(rms(x_ref[:ALIGN, :D].astype(F32), one), wk[...])[0:1, :].astype(BF16)

    def project(step, _):
        rows = pl.ds(pl.multiple_of(step * tile, tile), tile)
        normed = rms(x_ref[rows, :D].astype(F32), one)
        flag = live_ref[rows, :]
        q_ref[rows, :] = (dot(normed, wq[...]) * (HEAD_DIM**-0.5 * LOG2E)).astype(BF16)
        key = dot(normed, wk[...]).astype(BF16)
        k_ref[rows, :] = jnp.where(jnp.concatenate([flag, flag], axis=1) > 0, key, first)
        value = dot(normed, wv[...]).astype(BF16)
        for pair in range(HEADS // 2):
            part = value[:, pair * LANES : (pair + 1) * LANES]
            lanes = slice(pair * LANES, (pair + 1) * LANES)
            v_ref[2 * pair, rows, lanes] = jnp.where(low, part, flag)
            v_ref[2 * pair + 1, rows, lanes] = jnp.where(low, flag, part)
            other = slice((1 - pair) * LANES, (2 - pair) * LANES)
            v_ref[2 * pair, rows, other] = flag
            v_ref[2 * pair + 1, rows, other] = flag
        return 0

    lax.fori_loop(0, count // tile, project, 0)

    tile = asked[1]
    low = iota((tile, LANES), 1) < HEAD_DIM

    def attend(step, _):
        rows = slice(step * tile, (step + 1) * tile) if unroll else pl.ds(pl.multiple_of(step * tile, ALIGN), tile)

        def scored(head):
            lanes = slice(head // 2 * LANES, (head // 2 + 1) * LANES)
            query = q_ref[rows, lanes]
            own = jnp.where(low, query, zero) if head % 2 == 0 else jnp.where(low, zero, query)
            return dot_nt(own, k_ref[:count, lanes])

        def mixed(head, scores):
            peak = jnp.max(scores, axis=-1, keepdims=True)
            lanes = slice(head // 2 * LANES, (head // 2 + 1) * LANES)
            return dot(jnp.exp2(scores - peak).astype(BF16), v_ref[head, :count, :])[:, lanes]

        ahead = scored(0)
        outs = []
        for head in range(HEADS):
            scores = ahead
            if head + 1 < HEADS:
                ahead = scored(head + 1)
            outs.append(mixed(head, scores))
        parts = []
        for pair in range(HEADS // 2):
            even, odd = outs[2 * pair : 2 * pair + 2]
            total = pltpu.roll(jnp.where(low, odd, even), HEAD_DIM, 1)
            parts.append(jnp.where(low, even, odd) / total)
        att = jnp.concatenate(parts, axis=1).astype(BF16)
        hidden = x_ref[rows, :D].astype(F32) + dot(att, wo[...])
        up = gelu_twice(dot(rms(hidden, two), wu[...])).astype(BF16)
        y_ref[rows, :] = (hidden + 0.5 * dot(up, wd[...])).astype(BF16)
        return 0

    if unroll:
        for step in range(asked[0] // tile):
            attend(step, 0)
    else:
        lax.fori_loop(0, asked[0] // tile, attend, 0)


def layer_a_kernel(x_ref, *refs):
    sources, out_hbm, weights = refs[:8], refs[8], refs[9:17]
    sems, left, out_ref, y_ref, *rest = refs[17:]
    moves = fetch(0, sources, weights, sems)
    tags = message_rows(x_ref, 0)
    picks = jnp.where(iota((CAP, LANES), 0) == iota((CAP, LANES), 1), 1.0, 0.0).astype(BF16)
    tag_row = interleave(dot_nt(picks, tags.astype(BF16)))
    tag_col = columns(tag_row, SLOTS)
    slot = (tag_row - 1.0) * CAP + ranks_of(tag_row, tag_col)
    slot = jnp.where(tag_row > 0.0, slot, -1.0).astype(I32)
    for move in moves:
        move.wait()
    live = jnp.where(tag_col > 0.0, 1.0, 0.0)
    layer(0, SLOTS, 2 * TILE, (SLOTS, 2 * TILE), True, x_ref, live, weights, y_ref, *rest)
    scatter_out(slot, y_ref[...], out_ref, out_hbm, left)


def before(flags):
    parts = flags.shape[1] // LANES
    square = jnp.concatenate([flags[:, p * LANES : (p + 1) * LANES] for p in range(parts)], axis=0)
    upper = jnp.where(iota((LANES, LANES), 0) < iota((LANES, LANES), 1), 1.0, 0.0).astype(BF16)
    inner = dot(square.astype(BF16), upper)
    held = jnp.zeros((1, 1), F32)
    rows = []
    for p in range(parts):
        rows.append(inner[p : p + 1, :] + held)
        held = held + jnp.sum(square[p : p + 1, :], axis=1, keepdims=True)
    return jnp.concatenate(rows, axis=1)


def plan_kernel(x_ref, place_ref, slot_ref, live_ref, total_ref, rounds_ref):
    tags = message_rows(x_ref, 0)
    rounds_ref[0] = jnp.max(jnp.where(iota((DEVICES, LANES), 1) == CAP, tags, 0.0)).astype(I32)
    counts = message_rows(x_ref, 1)
    lower = jnp.where(iota((DEVICES, DEVICES), 0) >= iota((DEVICES, DEVICES), 1), 1.0, 0.0).astype(BF16)
    running = dot(lower, counts.astype(BF16))
    homes = []
    for turn in range(CAP):
        home = jnp.sum(jnp.where(running <= turn, 1.0, 0.0), axis=0, keepdims=True)
        homes.append(jnp.where(home < DEVICES, home + 1.0, 0.0))
    tag = interleave(jnp.concatenate(homes, axis=0))
    live = jnp.where(tag > 0.0, 1.0, 0.0)
    total_ref[0] = jnp.sum(live).astype(I32)
    place = jnp.where(tag > 0.0, before(live), -1.0).astype(I32)
    place_ref[...] = jnp.broadcast_to(place, (8, SLOTS))
    tag_col = dot(onehot_rows(0, SLOTS, place), columns(tag, SLOTS).astype(BF16))
    tag_row = tag_col.T[0:1, :]
    rank = ranks_of(tag_row, tag_col)
    turn = jnp.floor(rank * (1.0 / RET))
    slot = (tag_row - 1.0) * RET + (rank - turn * RET) + turn * BACK
    slot = jnp.where(tag_row > 0.0, slot, -1.0).astype(I32)
    slot_ref[...] = jnp.broadcast_to(slot, (8, SLOTS))
    flag = jnp.where(iota((SLOTS, LANES), 0) == 0, 1.0, jnp.where(tag_col > 0.0, 1.0, 0.0))
    live_ref[...] = flag.astype(BF16)


def call_plan(rows):
    smem = pl.BlockSpec(memory_space=pltpu.SMEM)
    return pl.pallas_call(
        plan_kernel,
        out_shape=[
            jax.ShapeDtypeStruct((8, SLOTS), I32),
            jax.ShapeDtypeStruct((8, SLOTS), I32),
            jax.ShapeDtypeStruct((SLOTS, LANES), BF16),
            jax.ShapeDtypeStruct((1,), I32),
            jax.ShapeDtypeStruct((1,), I32),
        ],
        in_specs=[VMEM],
        out_specs=[VMEM, VMEM, VMEM, smem, smem],
        compiler_params=pltpu.CompilerParams(vmem_limit_bytes=24 * 2**20),
        cost_estimate=pl.CostEstimate(flops=2 * 10**9, bytes_accessed=2**20, transcendentals=0),
    )(rows)


def finish_b(count, tile, asked, x_ref, place_ref, slot_ref, flag_ref, packed_ref, weights, moves, refs):
    out_hbm, left, out_ref, y_ref, *rest = refs
    packed_ref[:count, :] = dot(onehot_rows(0, count, place_ref[0:1, :]), x_ref[...]).astype(BF16)
    if count < SLOTS:
        y_ref[asked[0] :, :] = jnp.zeros((SLOTS - asked[0], D), BF16)
    for move in moves:
        move.wait()
    layer(1, count, tile, asked, count < SLOTS, packed_ref, flag_ref[:count, :], weights, y_ref, *rest)
    scatter_out(slot_ref[0:1, :count], y_ref[:count, :], out_ref, out_hbm, left)


def layer_b_kernel(x_ref, place_ref, slot_ref, flag_ref, total_ref, *refs):
    sources, (out_hbm, y_ref) = refs[:8], refs[8:10]
    weights, (sems, left, out_ref, packed_ref, *rest) = refs[10:18], refs[18:]
    moves = fetch(1, sources, weights, sems)
    given = (x_ref, place_ref, slot_ref, flag_ref, packed_ref, weights, moves, (out_hbm, left, out_ref, y_ref, *rest))

    @pl.when(total_ref[0] <= LIKELY)
    def _():
        finish_b(FEW, FEW // 2, (LIKELY, LIKELY // 2), *given)

    @pl.when(total_ref[0] > LIKELY)
    def _():
        finish_b(SLOTS, TILE, (SLOTS, TILE), *given)


def call_layer(kernel, out_shape, rows, plan, weights):
    kernel_weights = [pltpu.VMEM(weight.shape[1:], BF16) for weight in weights[:6]]
    kernel_weights += [pltpu.VMEM(gain.shape, F32) for gain in weights[6:]]
    scratch = [
        pltpu.VMEM((SLOTS, D), BF16),
        pltpu.VMEM((SLOTS, D), BF16),
        pltpu.VMEM((SLOTS, D), BF16),
        pltpu.VMEM((HEADS, SLOTS, D), BF16),
        pltpu.VMEM((SLOTS, LANES), BF16),
    ]
    smem = pl.BlockSpec(memory_space=pltpu.SMEM)
    return pl.pallas_call(
        kernel,
        out_shape=out_shape,
        in_specs=[VMEM] + [smem if part.shape == (1,) else VMEM for part in plan]
        + [pl.BlockSpec(memory_space=pltpu.HBM)] * 8,
        out_specs=[pl.BlockSpec(memory_space=pltpu.HBM)] + [VMEM] * (len(out_shape) - 1),
        scratch_shapes=kernel_weights
        + [pltpu.SemaphoreType.DMA((8,)), pltpu.SemaphoreType.DMA((out_shape[0].shape[0] // CHUNK,))]
        + [pltpu.VMEM(out_shape[0].shape, BF16)]
        + scratch,
        compiler_params=pltpu.CompilerParams(vmem_limit_bytes=24 * 2**20),
        cost_estimate=pl.CostEstimate(flops=6 * 10**9, bytes_accessed=4 * 2**20, transcendentals=5 * 2**20),
    )(rows, *plan, *map(kept, weights))


def resend_kernel(turn_ref, y_ref, slot_ref, out_ref):
    slot = slot_ref[0:1, :] - turn_ref[0] * BACK
    for first in range(0, BACK, CHUNK):
        hot = onehot_rows(first, CHUNK, slot)
        out_ref[first : first + CHUNK, :] = dot(hot, y_ref[...]).astype(BF16)


def gathered(want, back_ref):
    parts = []
    for first in range(0, LEAVES, LANES):
        block = want[first : first + LANES, :]
        hot = jnp.concatenate(
            [
                jnp.where(block == iota((LANES, LANES), 1) + lanes, 1.0, 0.0).astype(BF16)
                for lanes in range(0, BACK, LANES)
            ],
            axis=1,
        )
        parts.append(dot(hot, back_ref[...]))
    return jnp.concatenate(parts, axis=0)


def regather_kernel(turn_ref, back_ref, want_ref, held_ref, out_ref):
    rows = gathered(want_ref[...] - turn_ref[0] * BACK, back_ref)
    out_ref[...] = (held_ref[...].astype(F32) + rows).astype(BF16)


def order_kernel(ret_ref, parent_ref, want_ref, again_ref, block_ref, start_ref, held_ref):
    held_ref[...] = jnp.zeros(held_ref.shape, BF16)
    parent = parent_ref[...].astype(F32)
    ret = ret_ref[0:1, :].astype(F32)
    p_col = columns(parent, LEAVES)
    l_col = fiota((LEAVES, LANES), 0)
    parts = []
    for part in range(LEAVES // LANES):
        pr = parent[:, part * LANES : (part + 1) * LANES]
        lr = fiota((1, LANES), 1) + part * LANES
        less = jnp.where(p_col * LEAVES + l_col < pr * LEAVES + lr, 1.0, 0.0)
        parts.append(jnp.sum(less, axis=0, keepdims=True))
    place = jnp.concatenate(parts, axis=1)
    for first in range(0, LEAVES, LANES):
        rows = slice(first, first + LANES)
        hit = place == fiota((LANES, LEAVES), 0) + first
        want = jnp.sum(jnp.where(hit, ret, 0.0), axis=1, keepdims=True)
        want_ref[rows, :] = jnp.broadcast_to(want, (LANES, LANES)).astype(I32)
        again_ref[rows, :] = want_ref[rows, :]
        block = 2.0 * jnp.sum(jnp.where(hit, parent, 0.0), axis=1, keepdims=True)
        block_ref[rows, :] = jnp.broadcast_to(block, (LANES, LANES))
    block_ref[LEAVES:, :] = jnp.full((GROUP, LANES), -8.0, F32)
    below = jnp.where(p_col < fiota((1, LANES), 1) * LANES, 1.0, 0.0)
    start_ref[...] = jnp.broadcast_to(jnp.sum(below, axis=0, keepdims=True), (8, LANES)).astype(I32)


def call_order(ret, parent):
    return pl.pallas_call(
        order_kernel,
        out_shape=[
            jax.ShapeDtypeStruct((LEAVES, LANES), I32),
            jax.ShapeDtypeStruct((LEAVES, LANES), I32),
            jax.ShapeDtypeStruct((LEAVES + GROUP, LANES), F32),
            jax.ShapeDtypeStruct((8, LANES), I32),
            jax.ShapeDtypeStruct((LEAVES, D), BF16),
        ],
        in_specs=[VMEM, VMEM],
        out_specs=[VMEM] * 5,
        compiler_params=pltpu.CompilerParams(vmem_limit_bytes=24 * 2**20),
        cost_estimate=pl.CostEstimate(flops=10**9, bytes_accessed=2**20, transcendentals=0),
    )(ret, parent)


STRIP = 8


def conv_kernel(count, main_ref, above_ref, below_ref, head_ref, foot_ref, weight_ref, out_ref, w_ref):
    step = pl.program_id(0)

    @pl.when(step == 0)
    def _():
        zero = jnp.zeros((LANES, LANES), BF16)
        for b in range(3):
            for row in range(4):
                for r in range(2):
                    block = weight_ref[row - r, b] if 0 <= row - r < 3 else zero
                    w_ref[b, row * LANES : (row + 1) * LANES, r * LANES : (r + 1) * LANES] = block

    above = jnp.where(step == 0, head_ref[0, 0], above_ref[0, 0])
    below = jnp.where(step == count - 1, foot_ref[0, 0], below_ref[0, 0])
    rows = [above] + [main_ref[0, r] for r in range(STRIP)] + [below]
    column = iota((TILE, TILE), 0)
    for pair in range(STRIP // 2):
        wide = jnp.concatenate(rows[2 * pair : 2 * pair + 4], axis=1)
        left = pltpu.roll(dot(wide, w_ref[0]), 1, 0)
        right = pltpu.roll(dot(wide, w_ref[2]), TILE - 1, 0)
        both = dot(wide, w_ref[1])
        both = both + jnp.where(column == 0, 0.0, left) + jnp.where(column == TILE - 1, 0.0, right)
        out_ref[0, 2 * pair] = both[:, :LANES].astype(BF16)
        out_ref[0, 2 * pair + 1] = both[:, LANES:].astype(BF16)


def call_conv(coarse, head, foot, weight):
    rows, cols, channels = coarse.shape[1:]
    count = rows // STRIP
    single = (1, 1, cols, channels)
    return pl.pallas_call(
        functools.partial(conv_kernel, count),
        grid=(count,),
        out_shape=jax.ShapeDtypeStruct(coarse.shape, BF16),
        in_specs=[
            pl.BlockSpec((1, STRIP, cols, channels), lambda i: (0, i, 0, 0)),
            pl.BlockSpec(single, lambda i: (0, jnp.maximum(i * STRIP - 1, 0), 0, 0)),
            pl.BlockSpec(single, lambda i: (0, jnp.minimum(i * STRIP + STRIP, rows - 1), 0, 0)),
            pl.BlockSpec(single, lambda i: (0, 0, 0, 0)),
            pl.BlockSpec(single, lambda i: (0, 0, 0, 0)),
            pl.BlockSpec(weight.shape, lambda i: (0, 0, 0, 0)),
        ],
        out_specs=pl.BlockSpec((1, STRIP, cols, channels), lambda i: (0, i, 0, 0)),
        scratch_shapes=[pltpu.VMEM((3, 4 * LANES, 2 * LANES), BF16)],
        compiler_params=pltpu.CompilerParams(vmem_limit_bytes=24 * 2**20),
        cost_estimate=pl.CostEstimate(flops=6 * 10**9, bytes_accessed=8 * 2**20, transcendentals=0),
    )(*[kept(coarse)] * 3, head, foot, weight)


def field_kernel(start_ref, conv_hbm, held_hbm, rounds_ref, back_ref, want_ref, block_ref, we_ref, wp_ref, out_ref, pix_ref, conv_ref, held_ref, sems, held_sem):
    step = pl.program_id(0)

    def move(part):
        rows = pl.ds(part * BAND, BAND)
        return pltpu.make_async_copy(conv_hbm.at[0, rows], conv_ref.at[rows], sems.at[part])

    @pl.when(step == 0)
    def _():
        for part in range(conv_ref.shape[0] // BAND):
            move(part).start()
        held_ref[...] = jnp.zeros(held_ref.shape, BF16)

        @pl.when(rounds_ref[0] > 1)
        def _():
            load = pltpu.make_async_copy(held_hbm, held_ref, held_sem.at[0])
            load.start()
            load.wait()

        leaf = (gathered(want_ref[...], back_ref) + held_ref[...].astype(F32)).astype(BF16)
        expanded = gelu_twice(dot(leaf, we_ref[...])).astype(BF16)
        pixels = (0.5 * dot(expanded, wp_ref[...])).astype(BF16)
        for c in range(2):
            for r in range(2):
                lanes = slice(r * LANES, (r + 1) * LANES)
                pix_ref[c, :LEAVES, lanes] = pixels[:, (2 * r + c) * LANES : (2 * r + c + 1) * LANES]
            pix_ref[c, LEAVES:, :] = jnp.zeros((GROUP, D), BF16)

    def added(index, first):
        rows = pl.ds(pl.multiple_of(first, ALIGN), GROUP)
        spots = block_ref[rows, :].T[0:1, :] - (index * TILE).astype(F32)
        spots = jnp.concatenate([spots, spots + 1.0], axis=1).astype(I32)
        hot = jnp.where(iota((TILE, 2 * GROUP), 0) == spots, 1.0, 0.0).astype(BF16)
        return dot(hot, jnp.concatenate([pix_ref[0, rows, :], pix_ref[1, rows, :]], axis=0))

    def held_rows(pair):
        row = step * BAND + 2 * pair
        return jnp.concatenate([conv_ref[row], conv_ref[row + 1]], axis=1).astype(F32)

    def store(pair, total):
        out_ref[0, 2 * pair] = total[:, :LANES].astype(BF16)
        out_ref[0, 2 * pair + 1] = total[:, LANES:].astype(BF16)

    move(step).wait()
    crowded = False
    pairs = []
    for pair in range(BAND // 2):
        index = step * (BAND // 2) + pair
        first = start_ref[0, index] // ALIGN * ALIGN
        end = start_ref[0, index + 1]
        crowded = (end > first + GROUP) | crowded
        pairs.append((pair, index, first, end))
        store(pair, held_rows(pair) + added(index, first))

    @pl.when(crowded)
    def _():
        for pair, index, first, end in pairs:
            more = lambda part, total, index=index, first=first: total + added(index, first + part * GROUP)
            store(pair, lax.fori_loop(0, (end - first + GROUP - 1) // GROUP, more, held_rows(pair)))


def call_field(starts, conv, held, rounds, back, want, block, w_expand, w_pixels):
    rows, cols, channels = conv.shape[1:]
    strip = pl.BlockSpec((1, BAND, cols, channels), lambda i, s: (0, i, 0, 0))
    return pl.pallas_call(
        field_kernel,
        grid_spec=pltpu.PrefetchScalarGridSpec(
            num_scalar_prefetch=1,
            grid=(rows // BAND,),
            in_specs=[
                pl.BlockSpec(memory_space=pltpu.HBM),
                pl.BlockSpec(memory_space=pltpu.HBM),
                pl.BlockSpec(memory_space=pltpu.SMEM),
            ]
            + [VMEM] * 5,
            out_specs=strip,
            scratch_shapes=[
                pltpu.VMEM((2, LEAVES + GROUP, D), BF16),
                pltpu.VMEM(conv.shape[1:], BF16),
                pltpu.VMEM((LEAVES, D), BF16),
                pltpu.SemaphoreType.DMA((rows // BAND,)),
                pltpu.SemaphoreType.DMA((1,)),
            ],
        ),
        out_shape=jax.ShapeDtypeStruct(conv.shape, BF16),
        compiler_params=pltpu.CompilerParams(vmem_limit_bytes=32 * 2**20),
        cost_estimate=pl.CostEstimate(flops=2 * 10**9, bytes_accessed=10 * 2**20, transcendentals=2**17),
    )(starts, kept(conv), kept(held), rounds, back, want, block, w_expand, w_pixels)


def exchange(rows, capacity):
    width = rows.shape[1]
    blocks = rows.reshape(DEVICES, capacity, width)
    moved = lax.all_to_all(blocks, ("tile", "intra"), split_axis=0, concat_axis=0, tiled=True)
    return moved.reshape(DEVICES * capacity, width)


def shards(
    leaves,
    window_a,
    window_b,
    parent,
    coarse,
    w_query,
    w_key,
    w_value,
    w_out,
    w_up,
    w_down,
    gain_attn,
    gain_mlp,
    w_expand,
    w_pixels,
    conv_weight,
):
    weights = (w_query, w_key, w_value, w_out, w_up, w_down, gain_attn, gain_mlp)
    count = lax.axis_size("intra")
    rows = coarse.shape[1]
    head = lax.ppermute(coarse[:, rows - 1 :], "intra", [(i, i + 1) for i in range(count - 1)])
    foot = lax.ppermute(coarse[:, :1], "intra", [(i + 1, i) for i in range(count - 1)])
    sent, ret = pl.pallas_call(
        send_kernel,
        out_shape=[jax.ShapeDtypeStruct((SLOTS, WIDE), BF16), jax.ShapeDtypeStruct((8, LEAVES), I32)],
        in_specs=[pl.BlockSpec(memory_space=pltpu.HBM)] * 3,
        out_specs=[pl.BlockSpec(memory_space=pltpu.HBM), VMEM],
        scratch_shapes=[
            pltpu.VMEM((SLOTS, WIDE), BF16),
            pltpu.VMEM((LEAVES, D), BF16),
            pltpu.VMEM((1, LEAVES), I32),
            pltpu.VMEM((1, LEAVES), I32),
            pltpu.SemaphoreType.DMA((3,)),
            pltpu.SemaphoreType.DMA((SLOTS // CHUNK,)),
        ],
        compiler_params=pltpu.CompilerParams(vmem_limit_bytes=24 * 2**20),
        cost_estimate=pl.CostEstimate(flops=10**9, bytes_accessed=2**20, transcendentals=0),
    )(*map(kept, (leaves, window_a.reshape(1, LEAVES), window_b.reshape(1, LEAVES))))
    rows_a = exchange(sent, CAP)
    want, again_want, block, starts, held = call_order(ret, parent.reshape(1, LEAVES))
    rows_a, want, head, foot = lax.optimization_barrier((rows_a, want, head, foot))
    (sent_b,) = call_layer(layer_a_kernel, [jax.ShapeDtypeStruct((SLOTS, D), BF16)], rows_a, (), weights)
    rows_b = exchange(sent_b, CAP)
    place, slot, flag, live, rounds = call_plan(rows_a)
    home, y = call_layer(
        layer_b_kernel,
        [
            jax.ShapeDtypeStruct((BACK, D), BF16),
            jax.ShapeDtypeStruct((SLOTS, D), BF16),
        ],
        rows_b,
        (place, slot, flag, live),
        weights,
    )
    back = exchange(home, RET)
    total = rounds.reshape(())

    def more(state):
        return state[0] < total

    def again(state):
        turn, held = state
        index = turn.reshape(1)
        smem = pl.BlockSpec(memory_space=pltpu.SMEM)
        part = pl.pallas_call(
            resend_kernel,
            out_shape=jax.ShapeDtypeStruct((BACK, D), BF16),
            in_specs=[smem, VMEM, VMEM],
            out_specs=VMEM,
        )(index, y, slot)
        held = pl.pallas_call(
            regather_kernel,
            out_shape=jax.ShapeDtypeStruct((LEAVES, D), BF16),
            in_specs=[smem, VMEM, VMEM, VMEM],
            out_specs=VMEM,
        )(index, exchange(part, RET), again_want, held)
        return turn + 1, held

    _, held = lax.while_loop(more, again, (jnp.asarray(1, I32), held))
    head, held = lax.optimization_barrier((head, held))
    conv = call_conv(coarse, head, foot, conv_weight)
    return call_field(starts, conv, held, rounds, back, want, block, w_expand, w_pixels)


def solution(mesh):
    placed = (
        P(("tile", "intra"), None),
        P(("tile", "intra")),
        P(("tile", "intra")),
        P(("tile", "intra")),
        P("tile", "intra", None, None),
    ) + (P(),) * 11
    return jax.shard_map(
        shards,
        mesh=mesh,
        in_specs=placed,
        out_specs=P("tile", "intra", None, None),
        check_vma=False,
    )
```

```python
import functools
import math

import jax
import jax.numpy as jnp
from jax import lax
from jax.experimental import pallas as pl
from jax.experimental.pallas import tpu as pltpu
from jax.sharding import PartitionSpec as P

HEADS = 4
HEAD_DIM = 64
EPSILON = 1e-06
NEGATIVE = -1e30
LOG2E = math.log2(math.e)
GELU = math.sqrt(2.0 / math.pi)
D = 256
LANES = 128
WIDE = D + LANES
DEVICES = 128
CAP = 8
SLOTS = DEVICES * CAP
LEAVES = 512
RET = 16
BACK = DEVICES * RET
FEW = 640
LIKELY = 544
GROUP = 64
ALIGN = 16
CHUNK = 512
BAND = 16
TILE = 256
FF = 1024
F32 = jnp.float32
BF16 = jnp.bfloat16
I32 = jnp.int32

VMEM = pl.BlockSpec(memory_space=pltpu.VMEM)


def kept(array):
    return pltpu.with_memory_space_constraint(array, pltpu.HBM)


def iota(shape, dim):
    return lax.broadcasted_iota(I32, shape, dim)


def fiota(shape, dim):
    return iota(shape, dim).astype(F32)


def dot(a, b):
    return jnp.dot(a, b, preferred_element_type=F32)


def dot_nt(a, b):
    return lax.dot_general(a, b, (((1,), (1,)), ((), ())), preferred_element_type=F32)


def columns(row, count):
    return jnp.broadcast_to(row, (LANES, count)).T


def onehot_rows(first, rows, targets):
    want = iota((rows, targets.shape[1]), 0) + first
    return jnp.where(want == targets, 1.0, 0.0).astype(BF16)


def send_kernel(leaves_hbm, wa_hbm, wb_hbm, out_hbm, ret_ref, out_ref, leaves_ref, wa_ref, wb_ref, sems, left):
    moves = [
        pltpu.make_async_copy(source, target, sems.at[index])
        for index, (source, target) in enumerate(((wa_hbm, wa_ref), (wb_hbm, wb_ref), (leaves_hbm, leaves_ref)))
    ]
    for move in moves:
        move.start()
    moves[0].wait()
    moves[1].wait()
    a_row = wa_ref[...].astype(F32)
    b_row = wb_ref[...].astype(F32)
    a_col = columns(a_row, LEAVES)
    b_col = columns(b_row, LEAVES)
    l_col = fiota((LEAVES, LANES), 0)
    key_col = a_col * LEAVES + l_col
    slots = []
    ranks = []
    for part in range(LEAVES // LANES):
        lanes = slice(part * LANES, (part + 1) * LANES)
        ar = a_row[:, lanes]
        br = b_row[:, lanes]
        lr = fiota((1, LANES), 1) + part * LANES
        same_a = jnp.where(a_col == ar, jnp.where(l_col < lr, 1.0, 0.0), 0.0)
        same_b = jnp.where(b_col == br, jnp.where(key_col < ar * LEAVES + lr, 1.0, 0.0), 0.0)
        slots.append(ar * CAP + jnp.sum(same_a, axis=0, keepdims=True))
        ranks.append(jnp.sum(same_b, axis=0, keepdims=True))
    slot = jnp.concatenate(slots, axis=1).astype(I32)
    rank = jnp.concatenate(ranks, axis=1)
    turn = jnp.floor(rank * (1.0 / RET))
    ret = b_row * RET + (rank - turn * RET) + turn * BACK
    ret_ref[...] = jnp.broadcast_to(ret, (8, LEAVES)).astype(I32)
    rounds = jnp.max(turn) + 1.0
    lane = iota((LEAVES, LANES), 1)
    turn_col = columns(slot.astype(F32), LEAVES) - a_col * CAP
    held = jnp.where(turn_col == lane.astype(F32), b_col + 1.0, 0.0).astype(BF16)
    tags = dot(onehot_rows(0, DEVICES, a_row.astype(I32)), held)
    tags = jnp.where(iota((DEVICES, LANES), 1) == CAP, rounds, tags).astype(BF16)
    in_a = jnp.where(a_col == lane.astype(F32), 1.0, 0.0).astype(BF16)
    counts = dot(onehot_rows(0, DEVICES, b_row.astype(I32)), in_a).astype(BF16)
    line = iota((SLOTS, LANES), 0)
    spread = jnp.where(line // CAP == iota((SLOTS, LANES), 1), 1.0, 0.0).astype(BF16)
    extra = jnp.where(line % CAP == 0, dot(spread, tags), jnp.where(line % CAP == 1, dot(spread, counts), 0.0))
    out_ref[:, D:] = extra.astype(BF16)
    moves[2].wait()
    scatter_out(slot, leaves_ref[...], out_ref, out_hbm, left)


def message_rows(x_ref, which):
    pick = iota((DEVICES, SLOTS), 0) * CAP + which == iota((DEVICES, SLOTS), 1)
    return dot(jnp.where(pick, 1.0, 0.0).astype(BF16), x_ref[:, D:])


def interleave(by_turn):
    spread = jnp.where(iota((DEVICES, SLOTS), 1) // CAP == iota((DEVICES, SLOTS), 0), 1.0, 0.0).astype(BF16)
    wide = dot(by_turn.astype(BF16), spread)
    own = iota((CAP, SLOTS), 1) % CAP == iota((CAP, SLOTS), 0)
    return jnp.sum(jnp.where(own, wide, 0.0), axis=0, keepdims=True)


def ranks_of(tag_row, tag_col):
    ranks = []
    for part in range(tag_row.shape[1] // LANES):
        row = tag_row[:, part * LANES : (part + 1) * LANES]
        block = tag_col[part * LANES : (part + 1) * LANES, :]
        before = iota((LANES, LANES), 0) < iota((LANES, LANES), 1)
        hits = jnp.where(before, jnp.where(block == row, 1.0, 0.0), 0.0)
        rank = jnp.sum(hits, axis=0, keepdims=True)
        if part:
            above = jnp.where(tag_col[: part * LANES, :] == row, 1.0, 0.0)
            rank = rank + jnp.sum(above, axis=0, keepdims=True)
        ranks.append(rank)
    return jnp.concatenate(ranks, axis=1)


def rms(values, gain):
    mean_sq = jnp.mean(values * values, axis=-1, keepdims=True)
    return (values * lax.rsqrt(mean_sq + EPSILON) * gain).astype(BF16)


def scatter_out(slot, rows, held_ref, out_hbm, sems):
    moves = []
    for part in range(held_ref.shape[0] // CHUNK):
        lines = pl.ds(part * CHUNK, CHUNK)
        held_ref[lines, :D] = dot(onehot_rows(part * CHUNK, CHUNK, slot), rows).astype(BF16)
        moves.append(pltpu.make_async_copy(held_ref.at[lines], out_hbm.at[lines], sems.at[part]))
        moves[-1].start()
    for move in moves:
        move.wait()


def fetch(layer_index, sources, targets, sems):
    moves = []
    for index, (source, target) in enumerate(zip(sources, targets)):
        part = source if index >= 6 else source.at[layer_index]
        moves.append(pltpu.make_async_copy(part, target, sems.at[index]))
        moves[-1].start()
    return moves


def gelu_twice(x):
    inner = x * (x * x * (0.044715 * GELU) + GELU)
    return x + x * jnp.tanh(inner)


def layer(layer_index, count, tile, asked, unroll, x_ref, live, weights, y_ref, q_ref, k_ref, v_ref, live_ref):
    wq, wk, wv, wo, wu, wd, gain_one, gain_two = weights
    one = gain_one[layer_index : layer_index + 1, :]
    two = gain_two[layer_index : layer_index + 1, :]
    low = iota((tile, LANES), 1) < HEAD_DIM
    zero = jnp.asarray(0, BF16)
    live_ref[:count, :] = live.astype(BF16)
    first = dot(rms(x_ref[:ALIGN, :D].astype(F32), one), wk[...])[0:1, :].astype(BF16)

    def project(step, _):
        rows = pl.ds(step * tile if unroll and count == SLOTS else pl.multiple_of(step * tile, tile), tile)
        normed = rms(x_ref[rows, :D].astype(F32), one)
        flag = live_ref[rows, :]
        q_ref[rows, :] = (dot(normed, wq[...]) * (HEAD_DIM**-0.5 * LOG2E)).astype(BF16)
        key = dot(normed, wk[...]).astype(BF16)
        k_ref[rows, :] = jnp.where(jnp.concatenate([flag, flag], axis=1) > 0, key, first)
        value = dot(normed, wv[...]).astype(BF16)
        for pair in range(HEADS // 2):
            part = value[:, pair * LANES : (pair + 1) * LANES]
            lanes = slice(pair * LANES, (pair + 1) * LANES)
            v_ref[2 * pair, rows, lanes] = jnp.where(low, part, flag)
            v_ref[2 * pair + 1, rows, lanes] = jnp.where(low, flag, part)
            other = slice((1 - pair) * LANES, (2 - pair) * LANES)
            v_ref[2 * pair, rows, other] = flag
            v_ref[2 * pair + 1, rows, other] = flag
        return 0

    if unroll and count == SLOTS:
        for step in range(count // tile):
            project(step, 0)
    else:
        lax.fori_loop(0, count // tile, project, 0)

    tile = asked[1]
    low = iota((tile, LANES), 1) < HEAD_DIM

    def attend(step, _):
        rows = slice(step * tile, (step + 1) * tile) if unroll else pl.ds(pl.multiple_of(step * tile, ALIGN), tile)

        def scored(head):
            lanes = slice(head // 2 * LANES, (head // 2 + 1) * LANES)
            query = q_ref[rows, lanes]
            own = jnp.where(low, query, zero) if head % 2 == 0 else jnp.where(low, zero, query)
            return dot_nt(own, k_ref[:count, lanes])

        def mixed(head, scores):
            peak = jnp.max(scores, axis=-1, keepdims=True)
            lanes = slice(head // 2 * LANES, (head // 2 + 1) * LANES)
            return dot(jnp.exp2(scores - peak).astype(BF16), v_ref[head, :count, :])[:, lanes]

        ahead = scored(0)
        outs = []
        for head in range(HEADS):
            scores = ahead
            if head + 1 < HEADS:
                ahead = scored(head + 1)
            outs.append(mixed(head, scores))
        parts = []
        for pair in range(HEADS // 2):
            even, odd = outs[2 * pair : 2 * pair + 2]
            total = pltpu.roll(jnp.where(low, odd, even), HEAD_DIM, 1)
            parts.append(jnp.where(low, even, odd) / total)
        att = jnp.concatenate(parts, axis=1).astype(BF16)
        hidden = x_ref[rows, :D].astype(F32) + dot(att, wo[...])
        up = gelu_twice(dot(rms(hidden, two), wu[...])).astype(BF16)
        y_ref[rows, :] = (hidden + 0.5 * dot(up, wd[...])).astype(BF16)
        return 0

    if unroll:
        for step in range(asked[0] // tile):
            attend(step, 0)
    else:
        lax.fori_loop(0, asked[0] // tile, attend, 0)


def layer_a_kernel(x_ref, *refs):
    sources, out_hbm, weights = refs[:8], refs[8], refs[9:17]
    sems, left, out_ref, y_ref, *rest = refs[17:]
    moves = fetch(0, sources, weights, sems)
    tags = message_rows(x_ref, 0)
    picks = jnp.where(iota((CAP, LANES), 0) == iota((CAP, LANES), 1), 1.0, 0.0).astype(BF16)
    tag_row = interleave(dot_nt(picks, tags.astype(BF16)))
    tag_col = columns(tag_row, SLOTS)
    slot = (tag_row - 1.0) * CAP + ranks_of(tag_row, tag_col)
    slot = jnp.where(tag_row > 0.0, slot, -1.0).astype(I32)
    for move in moves:
        move.wait()
    live = jnp.where(tag_col > 0.0, 1.0, 0.0)
    layer(0, SLOTS, 2 * TILE, (SLOTS, 2 * TILE), True, x_ref, live, weights, y_ref, *rest)
    scatter_out(slot, y_ref[...], out_ref, out_hbm, left)


def before(flags):
    parts = flags.shape[1] // LANES
    square = jnp.concatenate([flags[:, p * LANES : (p + 1) * LANES] for p in range(parts)], axis=0)
    upper = jnp.where(iota((LANES, LANES), 0) < iota((LANES, LANES), 1), 1.0, 0.0).astype(BF16)
    inner = dot(square.astype(BF16), upper)
    held = jnp.zeros((1, 1), F32)
    rows = []
    for p in range(parts):
        rows.append(inner[p : p + 1, :] + held)
        held = held + jnp.sum(square[p : p + 1, :], axis=1, keepdims=True)
    return jnp.concatenate(rows, axis=1)


def plan_kernel(x_ref, place_ref, slot_ref, live_ref, total_ref, rounds_ref):
    tags = message_rows(x_ref, 0)
    rounds_ref[0] = jnp.max(jnp.where(iota((DEVICES, LANES), 1) == CAP, tags, 0.0)).astype(I32)
    counts = message_rows(x_ref, 1)
    lower = jnp.where(iota((DEVICES, DEVICES), 0) >= iota((DEVICES, DEVICES), 1), 1.0, 0.0).astype(BF16)
    running = dot(lower, counts.astype(BF16))
    homes = []
    for turn in range(CAP):
        home = jnp.sum(jnp.where(running <= turn, 1.0, 0.0), axis=0, keepdims=True)
        homes.append(jnp.where(home < DEVICES, home + 1.0, 0.0))
    tag = interleave(jnp.concatenate(homes, axis=0))
    live = jnp.where(tag > 0.0, 1.0, 0.0)
    total_ref[0] = jnp.sum(live).astype(I32)
    place = jnp.where(tag > 0.0, before(live), -1.0).astype(I32)
    place_ref[...] = jnp.broadcast_to(place, (8, SLOTS))
    tag_col = dot(onehot_rows(0, SLOTS, place), columns(tag, SLOTS).astype(BF16))
    tag_row = tag_col.T[0:1, :]
    rank = ranks_of(tag_row, tag_col)
    turn = jnp.floor(rank * (1.0 / RET))
    slot = (tag_row - 1.0) * RET + (rank - turn * RET) + turn * BACK
    slot = jnp.where(tag_row > 0.0, slot, -1.0).astype(I32)
    slot_ref[...] = jnp.broadcast_to(slot, (8, SLOTS))
    flag = jnp.where(iota((SLOTS, LANES), 0) == 0, 1.0, jnp.where(tag_col > 0.0, 1.0, 0.0))
    live_ref[...] = flag.astype(BF16)


def call_plan(rows):
    smem = pl.BlockSpec(memory_space=pltpu.SMEM)
    return pl.pallas_call(
        plan_kernel,
        out_shape=[
            jax.ShapeDtypeStruct((8, SLOTS), I32),
            jax.ShapeDtypeStruct((8, SLOTS), I32),
            jax.ShapeDtypeStruct((SLOTS, LANES), BF16),
            jax.ShapeDtypeStruct((1,), I32),
            jax.ShapeDtypeStruct((1,), I32),
        ],
        in_specs=[VMEM],
        out_specs=[VMEM, VMEM, VMEM, smem, smem],
        compiler_params=pltpu.CompilerParams(vmem_limit_bytes=24 * 2**20),
        cost_estimate=pl.CostEstimate(flops=2 * 10**9, bytes_accessed=2**20, transcendentals=0),
    )(rows)


def finish_b(count, tile, asked, x_ref, place_ref, slot_ref, flag_ref, packed_ref, weights, moves, refs):
    out_hbm, left, out_ref, y_ref, *rest = refs
    packed_ref[:count, :] = dot(onehot_rows(0, count, place_ref[0:1, :]), x_ref[...]).astype(BF16)
    if count < SLOTS:
        y_ref[asked[0] :, :] = jnp.zeros((SLOTS - asked[0], D), BF16)
    for move in moves:
        move.wait()
    layer(1, count, tile, asked, count < SLOTS, packed_ref, flag_ref[:count, :], weights, y_ref, *rest)
    scatter_out(slot_ref[0:1, :count], y_ref[:count, :], out_ref, out_hbm, left)


def layer_b_kernel(x_ref, place_ref, slot_ref, flag_ref, total_ref, *refs):
    sources, (out_hbm, y_ref) = refs[:8], refs[8:10]
    weights, (sems, left, out_ref, packed_ref, *rest) = refs[10:18], refs[18:]
    moves = fetch(1, sources, weights, sems)
    given = (x_ref, place_ref, slot_ref, flag_ref, packed_ref, weights, moves, (out_hbm, left, out_ref, y_ref, *rest))

    @pl.when(total_ref[0] <= LIKELY)
    def _():
        finish_b(FEW, FEW // 2, (LIKELY, LIKELY), *given)

    @pl.when(total_ref[0] > LIKELY)
    def _():
        finish_b(SLOTS, TILE, (SLOTS, TILE), *given)


def call_layer(kernel, out_shape, rows, plan, weights):
    kernel_weights = [pltpu.VMEM(weight.shape[1:], BF16) for weight in weights[:6]]
    kernel_weights += [pltpu.VMEM(gain.shape, F32) for gain in weights[6:]]
    scratch = [
        pltpu.VMEM((SLOTS, D), BF16),
        pltpu.VMEM((SLOTS, D), BF16),
        pltpu.VMEM((SLOTS, D), BF16),
        pltpu.VMEM((HEADS, SLOTS, D), BF16),
        pltpu.VMEM((SLOTS, LANES), BF16),
    ]
    smem = pl.BlockSpec(memory_space=pltpu.SMEM)
    return pl.pallas_call(
        kernel,
        out_shape=out_shape,
        in_specs=[VMEM] + [smem if part.shape == (1,) else VMEM for part in plan]
        + [pl.BlockSpec(memory_space=pltpu.HBM)] * 8,
        out_specs=[pl.BlockSpec(memory_space=pltpu.HBM)] + [VMEM] * (len(out_shape) - 1),
        scratch_shapes=kernel_weights
        + [pltpu.SemaphoreType.DMA((8,)), pltpu.SemaphoreType.DMA((out_shape[0].shape[0] // CHUNK,))]
        + [pltpu.VMEM(out_shape[0].shape, BF16)]
        + scratch,
        compiler_params=pltpu.CompilerParams(vmem_limit_bytes=24 * 2**20),
        cost_estimate=pl.CostEstimate(flops=6 * 10**9, bytes_accessed=4 * 2**20, transcendentals=5 * 2**20),
    )(rows, *plan, *map(kept, weights))


def resend_kernel(turn_ref, y_ref, slot_ref, out_ref):
    slot = slot_ref[0:1, :] - turn_ref[0] * BACK
    for first in range(0, BACK, CHUNK):
        hot = onehot_rows(first, CHUNK, slot)
        out_ref[first : first + CHUNK, :] = dot(hot, y_ref[...]).astype(BF16)


def gathered(want, back_ref):
    parts = []
    for first in range(0, LEAVES, LANES):
        block = want[first : first + LANES, :]
        hot = jnp.concatenate(
            [
                jnp.where(block == iota((LANES, LANES), 1) + lanes, 1.0, 0.0).astype(BF16)
                for lanes in range(0, BACK, LANES)
            ],
            axis=1,
        )
        parts.append(dot(hot, back_ref[...]))
    return jnp.concatenate(parts, axis=0)


def regather_kernel(turn_ref, back_ref, want_ref, held_ref, out_ref):
    rows = gathered(want_ref[...] - turn_ref[0] * BACK, back_ref)
    out_ref[...] = (held_ref[...].astype(F32) + rows).astype(BF16)


def order_kernel(ret_ref, parent_ref, want_ref, again_ref, block_ref, start_ref, held_ref):
    held_ref[...] = jnp.zeros(held_ref.shape, BF16)
    parent = parent_ref[...].astype(F32)
    ret = ret_ref[0:1, :].astype(F32)
    p_col = columns(parent, LEAVES)
    l_col = fiota((LEAVES, LANES), 0)
    parts = []
    for part in range(LEAVES // LANES):
        pr = parent[:, part * LANES : (part + 1) * LANES]
        lr = fiota((1, LANES), 1) + part * LANES
        less = jnp.where(p_col * LEAVES + l_col < pr * LEAVES + lr, 1.0, 0.0)
        parts.append(jnp.sum(less, axis=0, keepdims=True))
    place = jnp.concatenate(parts, axis=1)
    for first in range(0, LEAVES, LANES):
        rows = slice(first, first + LANES)
        hit = place == fiota((LANES, LEAVES), 0) + first
        want = jnp.sum(jnp.where(hit, ret, 0.0), axis=1, keepdims=True)
        want_ref[rows, :] = jnp.broadcast_to(want, (LANES, LANES)).astype(I32)
        again_ref[rows, :] = want_ref[rows, :]
        block = 2.0 * jnp.sum(jnp.where(hit, parent, 0.0), axis=1, keepdims=True)
        block_ref[rows, :] = jnp.broadcast_to(block, (LANES, LANES))
    block_ref[LEAVES:, :] = jnp.full((GROUP, LANES), -8.0, F32)
    below = jnp.where(p_col < fiota((1, LANES), 1) * LANES, 1.0, 0.0)
    start_ref[...] = jnp.broadcast_to(jnp.sum(below, axis=0, keepdims=True), (8, LANES)).astype(I32)


def call_order(ret, parent):
    return pl.pallas_call(
        order_kernel,
        out_shape=[
            jax.ShapeDtypeStruct((LEAVES, LANES), I32),
            jax.ShapeDtypeStruct((LEAVES, LANES), I32),
            jax.ShapeDtypeStruct((LEAVES + GROUP, LANES), F32),
            jax.ShapeDtypeStruct((8, LANES), I32),
            jax.ShapeDtypeStruct((LEAVES, D), BF16),
        ],
        in_specs=[VMEM, VMEM],
        out_specs=[VMEM] * 5,
        compiler_params=pltpu.CompilerParams(vmem_limit_bytes=24 * 2**20),
        cost_estimate=pl.CostEstimate(flops=10**9, bytes_accessed=2**20, transcendentals=0),
    )(ret, parent)


STRIP = 8


def conv_kernel(count, main_ref, above_ref, below_ref, head_ref, foot_ref, weight_ref, out_ref, w_ref):
    step = pl.program_id(0)

    @pl.when(step == 0)
    def _():
        zero = jnp.zeros((LANES, LANES), BF16)
        for b in range(3):
            for row in range(4):
                for r in range(2):
                    block = weight_ref[row - r, b] if 0 <= row - r < 3 else zero
                    w_ref[b, row * LANES : (row + 1) * LANES, r * LANES : (r + 1) * LANES] = block

    above = jnp.where(step == 0, head_ref[0, 0], above_ref[0, 0])
    below = jnp.where(step == count - 1, foot_ref[0, 0], below_ref[0, 0])
    rows = [above] + [main_ref[0, r] for r in range(STRIP)] + [below]
    column = iota((TILE, TILE), 0)
    for pair in range(STRIP // 2):
        wide = jnp.concatenate(rows[2 * pair : 2 * pair + 4], axis=1)
        left = pltpu.roll(dot(wide, w_ref[0]), 1, 0)
        right = pltpu.roll(dot(wide, w_ref[2]), TILE - 1, 0)
        both = dot(wide, w_ref[1])
        both = both + jnp.where(column == 0, 0.0, left) + jnp.where(column == TILE - 1, 0.0, right)
        out_ref[0, 2 * pair] = both[:, :LANES].astype(BF16)
        out_ref[0, 2 * pair + 1] = both[:, LANES:].astype(BF16)


def call_conv(coarse, head, foot, weight):
    rows, cols, channels = coarse.shape[1:]
    count = rows // STRIP
    single = (1, 1, cols, channels)
    return pl.pallas_call(
        functools.partial(conv_kernel, count),
        grid=(count,),
        out_shape=jax.ShapeDtypeStruct(coarse.shape, BF16),
        in_specs=[
            pl.BlockSpec((1, STRIP, cols, channels), lambda i: (0, i, 0, 0)),
            pl.BlockSpec(single, lambda i: (0, jnp.maximum(i * STRIP - 1, 0), 0, 0)),
            pl.BlockSpec(single, lambda i: (0, jnp.minimum(i * STRIP + STRIP, rows - 1), 0, 0)),
            pl.BlockSpec(single, lambda i: (0, 0, 0, 0)),
            pl.BlockSpec(single, lambda i: (0, 0, 0, 0)),
            pl.BlockSpec(weight.shape, lambda i: (0, 0, 0, 0)),
        ],
        out_specs=pl.BlockSpec((1, STRIP, cols, channels), lambda i: (0, i, 0, 0)),
        scratch_shapes=[pltpu.VMEM((3, 4 * LANES, 2 * LANES), BF16)],
        compiler_params=pltpu.CompilerParams(vmem_limit_bytes=24 * 2**20),
        cost_estimate=pl.CostEstimate(flops=6 * 10**9, bytes_accessed=8 * 2**20, transcendentals=0),
    )(*[kept(coarse)] * 3, head, foot, weight)


def field_kernel(start_ref, conv_hbm, held_hbm, rounds_ref, back_ref, want_ref, block_ref, we_ref, wp_ref, out_ref, pix_ref, conv_ref, held_ref, sems, held_sem):
    step = pl.program_id(0)

    def move(part):
        rows = pl.ds(part * BAND, BAND)
        return pltpu.make_async_copy(conv_hbm.at[0, rows], conv_ref.at[rows], sems.at[part])

    @pl.when(step == 0)
    def _():
        for part in range(conv_ref.shape[0] // BAND):
            move(part).start()
        held_ref[...] = jnp.zeros(held_ref.shape, BF16)

        @pl.when(rounds_ref[0] > 1)
        def _():
            load = pltpu.make_async_copy(held_hbm, held_ref, held_sem.at[0])
            load.start()
            load.wait()

        leaf = (gathered(want_ref[...], back_ref) + held_ref[...].astype(F32)).astype(BF16)
        expanded = gelu_twice(dot(leaf, we_ref[...])).astype(BF16)
        pixels = (0.5 * dot(expanded, wp_ref[...])).astype(BF16)
        for c in range(2):
            for r in range(2):
                lanes = slice(r * LANES, (r + 1) * LANES)
                pix_ref[c, :LEAVES, lanes] = pixels[:, (2 * r + c) * LANES : (2 * r + c + 1) * LANES]
            pix_ref[c, LEAVES:, :] = jnp.zeros((GROUP, D), BF16)

    def added(index, first):
        rows = pl.ds(pl.multiple_of(first, ALIGN), GROUP)
        spots = block_ref[rows, :].T[0:1, :] - (index * TILE).astype(F32)
        spots = jnp.concatenate([spots, spots + 1.0], axis=1).astype(I32)
        hot = jnp.where(iota((TILE, 2 * GROUP), 0) == spots, 1.0, 0.0).astype(BF16)
        return dot(hot, jnp.concatenate([pix_ref[0, rows, :], pix_ref[1, rows, :]], axis=0))

    def held_rows(pair):
        row = step * BAND + 2 * pair
        return jnp.concatenate([conv_ref[row], conv_ref[row + 1]], axis=1).astype(F32)

    def store(pair, total):
        out_ref[0, 2 * pair] = total[:, :LANES].astype(BF16)
        out_ref[0, 2 * pair + 1] = total[:, LANES:].astype(BF16)

    move(step).wait()
    crowded = False
    pairs = []
    for pair in range(BAND // 2):
        index = step * (BAND // 2) + pair
        first = start_ref[0, index] // ALIGN * ALIGN
        end = start_ref[0, index + 1]
        crowded = (end > first + GROUP) | crowded
        pairs.append((pair, index, first, end))
        store(pair, held_rows(pair) + added(index, first))

    @pl.when(crowded)
    def _():
        for pair, index, first, end in pairs:
            more = lambda part, total, index=index, first=first: total + added(index, first + part * GROUP)
            store(pair, lax.fori_loop(0, (end - first + GROUP - 1) // GROUP, more, held_rows(pair)))


def call_field(starts, conv, held, rounds, back, want, block, w_expand, w_pixels):
    rows, cols, channels = conv.shape[1:]
    strip = pl.BlockSpec((1, BAND, cols, channels), lambda i, s: (0, i, 0, 0))
    return pl.pallas_call(
        field_kernel,
        grid_spec=pltpu.PrefetchScalarGridSpec(
            num_scalar_prefetch=1,
            grid=(rows // BAND,),
            in_specs=[
                pl.BlockSpec(memory_space=pltpu.HBM),
                pl.BlockSpec(memory_space=pltpu.HBM),
                pl.BlockSpec(memory_space=pltpu.SMEM),
            ]
            + [VMEM] * 5,
            out_specs=strip,
            scratch_shapes=[
                pltpu.VMEM((2, LEAVES + GROUP, D), BF16),
                pltpu.VMEM(conv.shape[1:], BF16),
                pltpu.VMEM((LEAVES, D), BF16),
                pltpu.SemaphoreType.DMA((rows // BAND,)),
                pltpu.SemaphoreType.DMA((1,)),
            ],
        ),
        out_shape=jax.ShapeDtypeStruct(conv.shape, BF16),
        compiler_params=pltpu.CompilerParams(vmem_limit_bytes=32 * 2**20),
        cost_estimate=pl.CostEstimate(flops=2 * 10**9, bytes_accessed=10 * 2**20, transcendentals=2**17),
    )(starts, kept(conv), kept(held), rounds, back, want, block, w_expand, w_pixels)


def exchange(rows, capacity):
    width = rows.shape[1]
    blocks = rows.reshape(DEVICES, capacity, width)
    moved = lax.all_to_all(blocks, ("tile", "intra"), split_axis=0, concat_axis=0, tiled=True)
    return moved.reshape(DEVICES * capacity, width)


def shards(
    leaves,
    window_a,
    window_b,
    parent,
    coarse,
    w_query,
    w_key,
    w_value,
    w_out,
    w_up,
    w_down,
    gain_attn,
    gain_mlp,
    w_expand,
    w_pixels,
    conv_weight,
):
    weights = (w_query, w_key, w_value, w_out, w_up, w_down, gain_attn, gain_mlp)
    count = lax.axis_size("intra")
    rows = coarse.shape[1]
    head = lax.ppermute(coarse[:, rows - 1 :], "intra", [(i, i + 1) for i in range(count - 1)])
    foot = lax.ppermute(coarse[:, :1], "intra", [(i + 1, i) for i in range(count - 1)])
    sent, ret = pl.pallas_call(
        send_kernel,
        out_shape=[jax.ShapeDtypeStruct((SLOTS, WIDE), BF16), jax.ShapeDtypeStruct((8, LEAVES), I32)],
        in_specs=[pl.BlockSpec(memory_space=pltpu.HBM)] * 3,
        out_specs=[pl.BlockSpec(memory_space=pltpu.HBM), VMEM],
        scratch_shapes=[
            pltpu.VMEM((SLOTS, WIDE), BF16),
            pltpu.VMEM((LEAVES, D), BF16),
            pltpu.VMEM((1, LEAVES), I32),
            pltpu.VMEM((1, LEAVES), I32),
            pltpu.SemaphoreType.DMA((3,)),
            pltpu.SemaphoreType.DMA((SLOTS // CHUNK,)),
        ],
        compiler_params=pltpu.CompilerParams(vmem_limit_bytes=24 * 2**20),
        cost_estimate=pl.CostEstimate(flops=10**9, bytes_accessed=2**20, transcendentals=0),
    )(*map(kept, (leaves, window_a.reshape(1, LEAVES), window_b.reshape(1, LEAVES))))
    rows_a = exchange(sent, CAP)
    want, again_want, block, starts, held = call_order(ret, parent.reshape(1, LEAVES))
    rows_a, want, head, foot = lax.optimization_barrier((rows_a, want, head, foot))
    (sent_b,) = call_layer(layer_a_kernel, [jax.ShapeDtypeStruct((SLOTS, D), BF16)], rows_a, (), weights)
    rows_b = exchange(sent_b, CAP)
    place, slot, flag, live, rounds = call_plan(rows_a)
    home, y = call_layer(
        layer_b_kernel,
        [
            jax.ShapeDtypeStruct((BACK, D), BF16),
            jax.ShapeDtypeStruct((SLOTS, D), BF16),
        ],
        rows_b,
        (place, slot, flag, live),
        weights,
    )
    back = exchange(home, RET)
    total = rounds.reshape(())

    def more(state):
        return state[0] < total

    def again(state):
        turn, held = state
        index = turn.reshape(1)
        smem = pl.BlockSpec(memory_space=pltpu.SMEM)
        part = pl.pallas_call(
            resend_kernel,
            out_shape=jax.ShapeDtypeStruct((BACK, D), BF16),
            in_specs=[smem, VMEM, VMEM],
            out_specs=VMEM,
        )(index, y, slot)
        held = pl.pallas_call(
            regather_kernel,
            out_shape=jax.ShapeDtypeStruct((LEAVES, D), BF16),
            in_specs=[smem, VMEM, VMEM, VMEM],
            out_specs=VMEM,
        )(index, exchange(part, RET), again_want, held)
        return turn + 1, held

    _, held = lax.while_loop(more, again, (jnp.asarray(1, I32), held))
    head, held = lax.optimization_barrier((head, held))
    conv = call_conv(coarse, head, foot, conv_weight)
    return call_field(starts, conv, held, rounds, back, want, block, w_expand, w_pixels)


def solution(mesh):
    placed = (
        P(("tile", "intra"), None),
        P(("tile", "intra")),
        P(("tile", "intra")),
        P(("tile", "intra")),
        P("tile", "intra", None, None),
    ) + (P(),) * 11
    return jax.shard_map(
        shards,
        mesh=mesh,
        in_specs=placed,
        out_specs=P("tile", "intra", None, None),
        check_vma=False,
    )
```
